512 devices in a mesh: row: 16 (over z), col: 32 (over x, y, core).
Axes of the slice: x: 4, y: 4, z: 16, core: 2. Of those that a mesh axis runs over, the one named last changes fastest.
Arguments:
- gate_pre: bfloat16 [2048, 16384], P('row', 'col'), may hold values from -6 to 6
- up_pre: bfloat16 [2048, 16384], P('row', 'col'), may hold values from -6 to 6
- down_weight: bfloat16 [8192, 16384], P('row', 'col'), may hold values from -0.125 to 0.125
- block_mask: int32 [64, 128], P('row', 'col'), may hold values from 0 to 1, as said below
- cotangent: bfloat16 [2048, 8192], P('row', 'col'), may hold values from -6 to 6
Outputs:
- output: bfloat16 [2048, 8192], P('row', 'col')
- d_gate: bfloat16 [2048, 16384], P('row', 'col')
- d_up: bfloat16 [2048, 16384], P('row', 'col')
- d_down: bfloat16 [8192, 16384], P('row', 'col')
The draws below stay inside these ranges and needn't reach their ends.
Inputs may be any that keep to these rules, and one draw needn't show every extreme that they name: `block_mask`: each device's tile of 4 x 4 blocks keeps between 4 and 12 blocks; in every draw some tile keeps exactly 12.
All inputs are finite; a program needn't handle non-finite values.
Results may differ from the reference program's by a relative error of at most 0.015.
Values may be sent and summed in bfloat16 or wider, within the bound.
A program may use at most 64 MiB of HBM per device.

```python
import jax
import jax.numpy as jnp
from jax import lax

D = 8192
FF = 16384
BLK = 128
TOKENS = 2048
MASK_R = 64
MASK_C = 128
TILE_R = 4
TILE_C = 4
CAP = 12
N_ROW = 16
N_COL = 32


def draw_block_mask(key, part):
    grid_rows = MASK_R // TILE_R
    grid_cols = MASK_C // TILE_C
    tiles = grid_rows * grid_cols
    block_count = TILE_R * TILE_C
    key_counts, key_top, key_perm = jax.random.split(jax.random.fold_in(key, 17), 3)
    counts = jax.random.randint(key_counts, (tiles,), block_count // 4, CAP + 1)
    top_tile = jax.random.randint(key_top, (), 0, tiles)
    counts = jnp.where(jnp.arange(tiles) == top_tile, CAP, counts)
    perm_keys = jax.random.split(key_perm, tiles)
    perms = jax.vmap(lambda single: jax.random.permutation(single, block_count))(perm_keys)
    kept = (perms < counts[:, None]).astype(jnp.int32)
    shaped = kept.reshape(grid_rows, grid_cols, TILE_R, TILE_C).transpose(0, 2, 1, 3)
    return shaped.reshape(MASK_R, MASK_C)


def strengthened(array, key, source, target, blocks, factor):
    owner, partner = [(jnp.arange(array.shape[axis_at]) // (array.shape[axis_at] // blocks)).reshape([-1 if axis == axis_at else 1 for axis in range(array.ndim)]) for axis_at in (source, target)]
    chosen = jax.random.permutation(key, blocks)[partner]
    strong = (owner == chosen) | (owner == (partner + blocks // 2) % blocks)
    return jnp.where(strong, factor * array, array)


def block_levels(own_key, extent, cuts, smallest, top_value):
    level = 1.0
    for dim, parts in cuts:
        steps = jax.random.uniform(jax.random.fold_in(jax.random.fold_in(own_key, 6), dim), (parts,), jnp.float32, smallest / len(cuts), top_value / len(cuts))
        level = level * jnp.repeat(jnp.exp(steps), extent[dim] // parts).reshape((-1,) + (1,) * (len(extent) - 1 - dim))
    return level


def noise(stream_key, extent, deviation, reach, pieces=(), dtype=jnp.bfloat16):
    result = jax.random.normal(stream_key, extent, jnp.float32) * deviation
    if len(pieces) > 0:
        result = block_levels(stream_key, extent, pieces, -0.22, 0.18) * result
    return jnp.clip(result, min=-reach, max=reach).astype(dtype)


def bell_draw_with(key, shape, spread, limit, cuts, heavy, dtype=jnp.bfloat16):
    array = spread * jax.random.normal(key, shape, jnp.float32)
    if cuts:
        array = array * block_levels(key, shape, cuts, -0.22, 0.18)
    return jnp.clip(strengthened(array, jax.random.fold_in(key, 3), *heavy), -limit, limit).astype(dtype)


def setup_inputs(seed: int = 0) -> dict:
    streams_of = jax.random.split(jax.random.key(seed), 6)
    gate_pre = noise(streams_of[0], (TOKENS, FF), 1.0, 6.0, ((0, 16), (1, 32)))
    up_pre = noise(streams_of[1], (TOKENS, FF), 1.0, 6.0, ((0, 16), (1, 32)))
    down_weight = bell_draw_with(streams_of[2], (D, FF), (FF // 2) ** -0.5, 0.125, ((0, 16), (1, 32)), (1, 0, 32, 2.75))
    block_mask = draw_block_mask(jax.random.fold_in(streams_of[5], 71), 0)
    cotangent = noise(streams_of[4], (TOKENS, D), 1.0, 6.0, ((0, 16), (1, 32)))
    return dict(gate_pre=gate_pre, up_pre=up_pre, down_weight=down_weight, block_mask=block_mask, cotangent=cotangent)


def reference(gate_pre, up_pre, down_weight, block_mask, cotangent):
    gate_wide = gate_pre.astype(jnp.float32)
    up_wide = up_pre.astype(jnp.float32)
    activated = jax.nn.silu(gate_wide)
    hidden = (activated * up_wide).astype(jnp.bfloat16)
    expand = jnp.repeat(jnp.repeat(block_mask, BLK, axis=0), BLK, axis=1)
    masked = jnp.where(expand > 0, down_weight, jnp.zeros_like(down_weight))
    group = FF // N_COL
    total = jnp.zeros((TOKENS, D), jnp.float32)
    for column in range(N_COL):
        lhs = hidden[:, column * group:(column + 1) * group]
        rhs = masked[:, column * group:(column + 1) * group]
        part = lax.dot_general(lhs, rhs, (((1,), (1,)), ((), ())), preferred_element_type=jnp.float32)
        part = lax.optimization_barrier(part.astype(jnp.bfloat16))
        total = total + part.astype(jnp.float32)
    output = total.astype(jnp.bfloat16)
    width_group = D // N_ROW
    d_hidden = jnp.zeros((TOKENS, FF), jnp.float32)
    for rowgroup in range(N_ROW):
        lhs = cotangent[:, rowgroup * width_group:(rowgroup + 1) * width_group]
        rhs = masked[rowgroup * width_group:(rowgroup + 1) * width_group, :]
        back = jnp.dot(lhs, rhs, preferred_element_type=jnp.float32)
        back = lax.optimization_barrier(back.astype(jnp.bfloat16))
        d_hidden = d_hidden + back.astype(jnp.float32)
    sigmoid_g = jax.nn.sigmoid(gate_wide)
    d_gate = (d_hidden * up_wide * sigmoid_g * (1.0 + gate_wide * (1.0 - sigmoid_g))).astype(jnp.bfloat16)
    d_up = (d_hidden * activated).astype(jnp.bfloat16)
    grad_full = lax.dot_general(cotangent, hidden, (((0,), (0,)), ((), ())), preferred_element_type=jnp.float32)
    d_down = jnp.where(expand > 0, grad_full, jnp.zeros_like(grad_full)).astype(jnp.bfloat16)
    return output, d_gate, d_up, d_down
```

```python
import functools

import jax
import jax.numpy as jnp
from jax import lax
from jax.experimental import pallas as pl
from jax.experimental.pallas import tpu as pltpu
from jax.sharding import PartitionSpec as P

MESH = pl.DeviceIdType.MESH
SUB = 4
GRP = 4
TR = 16
TC = 128
F32 = jnp.float32
BF16 = jnp.bfloat16


def nt_dot(a, b):
    return lax.dot_general(a, b, (((1,), (1,)), ((), ())), preferred_element_type=F32)


def tn_dot(a, b):
    return lax.dot_general(a, b, (((0,), (0,)), ((), ())), preferred_element_type=F32)


def kernel(nz, nq, gate_hbm, up_hbm, w_hbm, mask_ref, cot_hbm,
           out_ref, dgate_ref, dup_ref, ddown_ref,
           gate_v, up_v, wm, cot_v, hall, call, cA, cB,
           yown, ysend, yprt, ysum, yrecv, osum, oB, out_v,
           rbuf, sbuf, pbuf, acc,
           ld, ag_s, ag_r, rs_s, rs_r, cA_s, cA_r, cB_s, cB_r,
           cg_s, cg_r, rel_s, rel_r, yp_s, yp_r, yr_s, yr_r,
           oB_s, oB_r, ov_s, ov_r):
    z = lax.axis_index("row")
    col = lax.axis_index("col")
    p = lax.div(col, 2)
    c = lax.rem(col, 2)
    half = nz // 2
    tok, ffc = gate_v.shape
    dh_w = wm.shape[0] // 2
    rsub = tok // SUB
    per = nz // GRP

    def zmod(v):
        return lax.rem(v + 2 * nz, nz)

    def qmod(v):
        return lax.rem(v + 2 * nq, nq)

    def tile_rows(q):
        return pl.ds(pl.multiple_of(lax.div(q, 2) * TR, TR), TR)

    def tile_cols(q, base=0):
        return pl.ds(pl.multiple_of(base + lax.rem(q, 2) * TC, TC), TC)

    def zdev(r):
        return (r, col)

    def qdev(q):
        return (z, q * 2 + c)

    pdev = (z, p * 2 + (1 - c))
    mine = pl.multiple_of(c * dh_w, TC)
    other = pl.multiple_of((1 - c) * dh_w, TC)

    def remote(src, dst, ss, rs, dev):
        return pltpu.make_async_remote_copy(
            src_ref=src, dst_ref=dst, send_sem=ss, recv_sem=rs,
            device_id=dev, device_id_type=MESH)

    def drain(ref, sem):
        pltpu.make_async_copy(ref, ref, sem).wait()

    bar = pltpu.get_barrier_semaphore()

    @pl.loop(1, nz)
    def _(k):
        pl.semaphore_signal(bar, inc=1, device_id=zdev(zmod(z + k)), device_id_type=MESH)

    @pl.loop(1, nq)
    def _(k):
        pl.semaphore_signal(bar, inc=1, device_id=qdev(qmod(p + k)), device_id_type=MESH)

    pl.semaphore_signal(bar, inc=1, device_id=pdev, device_id_type=MESH)

    loads = [pltpu.make_async_copy(a, b, ld.at[i]) for i, (a, b) in enumerate(
        ((gate_hbm, gate_v), (up_hbm, up_v), (cot_hbm, cot_v), (w_hbm, wm)))]
    for l in loads:
        l.start()
    loads[0].wait()
    loads[1].wait()
    g = gate_v[...].astype(F32)
    hall[z] = (g / (1.0 + jnp.exp(-g)) * up_v[...].astype(F32)).astype(BF16)
    loads[2].wait()
    loads[3].wait()
    br, bc = mask_ref.shape
    bs = wm.shape[0] // br
    for i in range(br):
        for j in range(bc):
            sl = (pl.ds(i * bs, bs), pl.ds(j * bs, bs))
            keep = jnp.full((bs, bs), mask_ref[i, j], jnp.int32) > 0
            wm[sl] = jnp.where(keep, wm[sl], jnp.zeros((bs, bs), BF16))
    pl.semaphore_wait(bar, nz + nq - 1)

    def steps_of(d, u):
        return half if (u < SUB // 2) == (d == 0) else half - 1

    pairs = [(d, u, 1 - 2 * d, steps_of(d, u)) for u in range(SUB) for d in range(2)]

    def ag(d, u, sg, s):
        ref = hall.at[zmod(z - sg * s), pl.ds(u * rsub, rsub)]
        return remote(ref, ref, ag_s.at[d, u, s], ag_r.at[d, u, s], zdev(zmod(z + sg)))

    def ag_wait(d, u, sg, s):
        ref = hall.at[zmod(z - sg * (s + 1)), pl.ds(u * rsub, rsub)]
        drain(ref, ag_r.at[d, u, s])

    def y_chunk(i, slot):
        h = hall[slot]
        ysend[i] = nt_dot(h, wm[pl.ds(other, dh_w), :]).astype(BF16)
        yown[i] = nt_dot(h, wm[pl.ds(mine, dh_w), :])
        remote(ysend.at[i], yprt.at[i], yp_s, yp_r.at[i], pdev).start()

    def y_pair(i):
        drain(yprt.at[i], yp_r.at[i])
        ysum[i] = (yown[i] + yprt[i].astype(F32)).astype(BF16)

    def y_scatter(n):
        rows = pl.ds(n * per, per)
        pltpu.make_async_copy(
            ysum.at[rows, tile_rows(p), tile_cols(p)], yrecv.at[p, rows], yr_r.at[n]).start()

        @pl.loop(1, nq)
        def _(k):
            q = qmod(p + k)
            remote(ysum.at[rows, tile_rows(q), tile_cols(q)], yrecv.at[p, rows],
                   yr_s.at[n], yr_r.at[n], qdev(q)).start()

    def y_finish(n):
        rows = pl.ds(n * per, per)
        drain(yrecv.at[:, rows], yr_r.at[n])
        osum[rows] = jnp.sum(yrecv[:, rows].astype(F32), axis=0).astype(BF16)
        for i in range(n * per, (n + 1) * per):
            off = -((i + 1) // 2) if i % 2 else i // 2
            if i == 0:
                pltpu.make_async_copy(osum.at[i], oB.at[z], oB_r).start()
            else:
                remote(osum.at[i], oB.at[z], oB_s, oB_r, zdev(zmod(z + off))).start()

    for d, u, sg, n in pairs:
        ag(d, u, sg, 0).start()

    pltpu.make_async_copy(cot_v.at[tile_rows(p), tile_cols(p)], cA.at[p], cA_r).start()

    @pl.loop(1, nq)
    def _(k):
        q = qmod(p + k)
        remote(cot_v.at[tile_rows(q), tile_cols(q)], cA.at[p], cA_s, cA_r, qdev(q)).start()

    y_chunk(0, z)

    def cot_two():
        drain(cA, cA_r)
        pltpu.make_async_copy(cA.at[z], cB.at[z], cB_r).start()

        @pl.loop(1, nz)
        def _(k):
            r = zmod(z + k)
            remote(cA.at[r], cB.at[z], cB_s, cB_r, zdev(r)).start()

    def cot_region(q):
        return call.at[:, tile_rows(q), tile_cols(q, mine)]

    def cot_three():
        drain(cB, cB_r)
        pltpu.make_async_copy(cB, cot_region(p), cg_r.at[0]).start()

        @pl.loop(1, nq)
        def _(k):
            remote(cB, cot_region(p), cg_s, cg_r.at[k], qdev(qmod(p + k))).start()

    @pl.loop(1, half)
    def _(s):
        for d, u, sg, n in pairs:
            ag_wait(d, u, sg, s - 1)
            if n == half:
                ag(d, u, sg, s).start()
            else:
                @pl.when(s < n)
                def _():
                    ag(d, u, sg, s).start()
        y_chunk(2 * s - 1, zmod(z - s))
        y_chunk(2 * s, zmod(z + s))
        y_pair(2 * s - 2)

        @pl.when(s > 1)
        def _():
            y_pair(2 * s - 3)

        @pl.when(s == 1)
        def _():
            cot_two()

        @pl.when(s == half // 2)
        def _():
            y_scatter(0)
            cot_three()

    for d, u, sg, n in pairs:
        if n == half:
            ag_wait(d, u, sg, half - 1)
    y_chunk(nz - 1, zmod(z + half))

    @pl.loop(0, nq)
    def _(k):
        ref = cot_region(qmod(p - k))
        drain(ref, cg_r.at[k])
        remote(ref, ref, rel_s, rel_r, pdev).start()

    drain(call.at[:, :, pl.ds(other, dh_w)], rel_r)

    def rs(d, u, sg, s):
        rows = pl.ds(u * rsub, rsub)
        return remote(sbuf.at[d, s, rows], rbuf.at[d, s, rows],
                      rs_s.at[d, u, s], rs_r.at[d, u, s], zdev(zmod(z + sg)))

    def part(d, s):
        t = zmod(z + (1 - 2 * d) * (half - s))
        pbuf[d] = jnp.dot(call[t], wm[...], preferred_element_type=F32)

    part(0, 0)
    for d, u, sg, n in pairs:
        if n == half:
            rows = pl.ds(u * rsub, rsub)
            sbuf[d, 0, rows] = pbuf[0, rows].astype(BF16)
    for d, u, sg, n in pairs:
        if n == half:
            rs(d, u, sg, 0).start()
    part(0, 1)
    part(1, 1)
    for i in (nz - 3, nz - 2, nz - 1):
        y_pair(i)
    for n in range(1, GRP):
        y_scatter(n)

    dw_events = {1: 0, 2: 1, 3: 2, 4: 3} if half > 4 else {1: 0}
    tgrp = nz // 4

    def dw(n):
        a = call[n * tgrp:(n + 1) * tgrp].reshape(tgrp * tok, wm.shape[0])
        b = hall[n * tgrp:(n + 1) * tgrp].reshape(tgrp * tok, ffc)
        v = tn_dot(a, b)
        if n == 0:
            acc[...] = v
        else:
            acc[...] += v

    def out_two():
        drain(oB, oB_r)
        pltpu.make_async_copy(oB.at[p], out_v.at[tile_rows(p), tile_cols(p)], ov_r).start()

        @pl.loop(1, nq)
        def _(k):
            q = qmod(p + k)
            remote(oB.at[q], out_v.at[tile_rows(p), tile_cols(p)], ov_s, ov_r, qdev(q)).start()

    @pl.loop(1, half)
    def _(s):
        for d, u, sg, n in pairs:
            rows = pl.ds(u * rsub, rsub)
            if n == half:
                drain(rbuf.at[d, s - 1, rows], rs_r.at[d, u, s - 1])
                sbuf[d, s, rows] = (pbuf[d, rows] + rbuf[d, s - 1, rows].astype(F32)).astype(BF16)
            else:
                @pl.when(s > 1)
                def _():
                    drain(rbuf.at[d, s - 1, rows], rs_r.at[d, u, s - 1])
                    sbuf[d, s, rows] = (pbuf[d, rows] + rbuf[d, s - 1, rows].astype(F32)).astype(BF16)

                @pl.when(s == 1)
                def _():
                    sbuf[d, s, rows] = pbuf[d, rows].astype(BF16)
            rs(d, u, sg, s).start()

        part(0, s + 1)

        @pl.when(s < half - 1)
        def _():
            part(1, s + 1)

        if half > 4:
            for at, n in {1: 0, 2: 1, 3: 2, 4: 3}.items():
                @pl.when(s == at)
                def _():
                    dw(n)
            for at, n in {3: 0, 4: 1, 5: 2, 6: 3}.items():
                @pl.when(s == at)
                def _():
                    y_finish(n)
        else:
            for n in range(4):
                dw(n)
                y_finish(n)

    out_two()
    for d, u, sg, n in pairs:
        drain(rbuf.at[d, half - 1, pl.ds(u * rsub, rsub)], rs_r.at[d, u, half - 1])
    for n in range(SUB):
        rows = pl.ds(n * rsub, rsub)
        dh = pbuf[0, rows] + rbuf[0, half - 1, rows].astype(F32) + rbuf[1, half - 1, rows].astype(F32)
        g = gate_v[rows, :].astype(F32)
        sig = 1.0 / (1.0 + jnp.exp(-g))
        dgate_ref[rows, :] = (dh * up_v[rows, :].astype(F32) * sig * (1.0 + g * (1.0 - sig))).astype(BF16)
        dup_ref[rows, :] = (dh * (g * sig)).astype(BF16)
    for i in range(br):
        for j in range(bc):
            sl = (pl.ds(i * bs, bs), pl.ds(j * bs, bs))
            keep = jnp.full((bs, bs), mask_ref[i, j], jnp.int32) > 0
            ddown_ref[sl] = jnp.where(keep, acc[sl], jnp.zeros((bs, bs), F32)).astype(BF16)

    for d, u, sg, n in pairs:
        @pl.loop(0, n)
        def _(s):
            drain(hall.at[0, pl.ds(0, rsub)], ag_s.at[d, u, s])

        @pl.loop(half - n, half)
        def _(s):
            drain(sbuf.at[d, s, pl.ds(u * rsub, rsub)], rs_s.at[d, u, s])
    rest = pl.ds(0, nq - 1)
    drain(cA.at[rest], cA_s)
    drain(cB.at[rest], cB_s)
    drain(call.at[rest, :, pl.ds(0, dh_w)], cg_s)
    drain(call.at[:, :, pl.ds(0, dh_w)], rel_s)
    drain(ysend, yp_s)
    for n in range(GRP):
        drain(yrecv.at[rest, pl.ds(n * per, per)], yr_s.at[n])
    drain(oB.at[rest], oB_s)
    drain(oB.at[rest], ov_s)
    drain(out_v, ov_r)
    out_ref[...] = out_v[...]


def body(nz, nq, gate_pre, up_pre, down_weight, block_mask, cotangent):
    tok, ffc = gate_pre.shape
    dr = down_weight.shape[0]
    dh_w = dr // 2
    half = nz // 2
    dma = pltpu.SemaphoreType.DMA
    vm = pltpu.VMEM
    any_ = pl.BlockSpec(memory_space=pl.ANY)
    vout = pl.BlockSpec(memory_space=pltpu.VMEM)
    return pl.pallas_call(
        functools.partial(kernel, nz, nq),
        out_shape=(
            jax.ShapeDtypeStruct((tok, dh_w), BF16),
            jax.ShapeDtypeStruct((tok, ffc), BF16),
            jax.ShapeDtypeStruct((tok, ffc), BF16),
            jax.ShapeDtypeStruct((dr, ffc), BF16),
        ),
        in_specs=[any_, any_, any_, pl.BlockSpec(memory_space=pltpu.SMEM), any_],
        out_specs=(vout,) * 4,
        scratch_shapes=[
            vm((tok, ffc), BF16), vm((tok, ffc), BF16), vm((dr, ffc), BF16), vm((tok, dh_w), BF16),
            vm((nz, tok, ffc), BF16), vm((nz, tok, dr), BF16),
            vm((nq, TR, TC), BF16), vm((nz, TR, TC), BF16),
            vm((nz, tok, dh_w), F32), vm((nz, tok, dh_w), BF16), vm((nz, tok, dh_w), BF16),
            vm((nz, tok, dh_w), BF16), vm((nq, nz, TR, TC), BF16),
            vm((nz, TR, TC), BF16), vm((nz, TR, TC), BF16), vm((tok, dh_w), BF16),
            vm((2, half, tok, ffc), BF16), vm((2, half, tok, ffc), BF16),
            vm((2, tok, ffc), F32), vm((dr, ffc), F32),
            dma((4,)), dma((2, SUB, half)), dma((2, SUB, half)), dma((2, SUB, half)), dma((2, SUB, half)),
            dma, dma, dma, dma,
            dma, dma((nq,)), dma, dma, dma, dma((nz,)), dma((GRP,)), dma((GRP,)),
            dma, dma, dma, dma,
        ],
        compiler_params=pltpu.CompilerParams(
            collective_id=0, has_side_effects=True, vmem_limit_bytes=60 * 1024 * 1024),
    )(gate_pre, up_pre, down_weight, block_mask, cotangent)


def solution(mesh):
    nz = mesh.shape["row"]
    nq = mesh.shape["col"] // 2
    spec = P("row", "col")
    return jax.shard_map(functools.partial(body, nz, nq), mesh=mesh, in_specs=(spec,) * 5,
                         out_specs=(spec,) * 4, check_vma=False)
```

```python
import functools

import jax
import jax.numpy as jnp
from jax import lax
from jax.experimental import pallas as pl
from jax.experimental.pallas import tpu as pltpu
from jax.sharding import PartitionSpec as P

MESH = pl.DeviceIdType.MESH
SUB = 4
TR = 16
TC = 128
F32 = jnp.float32
BF16 = jnp.bfloat16


def nt_dot(a, b):
    return lax.dot_general(a, b, (((1,), (1,)), ((), ())), preferred_element_type=F32)


def tn_dot(a, b):
    return lax.dot_general(a, b, (((0,), (0,)), ((), ())), preferred_element_type=F32)


def groups(nz):
    half = nz // 2
    if half <= 4:
        return [(i, i + 1) for i in range(nz)]
    cut = [0, 5, 9, 13, nz]
    return list(zip(cut[:-1], cut[1:]))


def kernel(nz, nq, gate_hbm, up_hbm, w_hbm, mask_ref, cot_hbm,
           out_hbm, dh_hbm, dw_hbm,
           gate_v, up_v, wm, cot_v, hall, call, cA, cB,
           yown, ysend, yprt, ysum, yrecv, osum, oB, out_v,
           rbuf, sbuf, pbuf, acc, accb,
           ld, ag_s, ag_r, rs_s, rs_r, cA_s, cA_r, cB_s, cB_r,
           cg_s, cg_r, rel_s, rel_r, yp_s, yp_r, yr_s, yr_r,
           oB_s, oB_r, ov_s, ov_r, st):
    z = lax.axis_index("row")
    col = lax.axis_index("col")
    p = lax.div(col, 2)
    c = lax.rem(col, 2)
    half = nz // 2
    tok, ffc = gate_v.shape
    dr = wm.shape[0]
    dw_h = dr // 2
    rsub = tok // SUB
    big = half > 4
    grps = groups(nz)

    def zdev(k):
        return (lax.rem(z + (k + nz), nz), col)

    def qmod(v):
        return lax.rem(v + nq, nq)

    def tile(q):
        return (pl.ds(pl.multiple_of(lax.div(q, 2) * TR, TR), TR),
                pl.ds(pl.multiple_of(lax.rem(q, 2) * TC, TC), TC))

    def qdev(q):
        return (z, q * 2 + c)

    pdev = (z, p * 2 + (1 - c))
    mine = pl.multiple_of(c * dw_h, TC)
    other = pl.multiple_of((1 - c) * dw_h, TC)

    def remote(src, dst, ss, rs, dev):
        return pltpu.make_async_remote_copy(
            src_ref=src, dst_ref=dst, send_sem=ss, recv_sem=rs,
            device_id=dev, device_id_type=MESH)

    def local(src, dst, sem):
        return pltpu.make_async_copy(src, dst, sem)

    def drain(ref, sem):
        pltpu.make_async_copy(ref, ref, sem).wait()

    bar = pltpu.get_barrier_semaphore()

    @pl.loop(1, nz)
    def _(k):
        pl.semaphore_signal(bar, inc=1, device_id=zdev(k), device_id_type=MESH)

    @pl.loop(1, nq)
    def _(k):
        pl.semaphore_signal(bar, inc=1, device_id=qdev(qmod(p + k)), device_id_type=MESH)

    pl.semaphore_signal(bar, inc=1, device_id=pdev, device_id_type=MESH)

    loads = [local(a, b, ld.at[i]) for i, (a, b) in enumerate((
        (gate_hbm, gate_v), (up_hbm, up_v), (cot_hbm, cot_v),
        (w_hbm.at[pl.ds(mine, dw_h)], wm.at[pl.ds(0, dw_h)]),
        (w_hbm.at[pl.ds(other, dw_h)], wm.at[pl.ds(dw_h, dw_h)])))]
    for l in loads:
        l.start()
    loads[0].wait()
    loads[1].wait()
    g = gate_v[...].astype(F32)
    hall[0] = (g / (1.0 + jnp.exp(-g)) * up_v[...].astype(F32)).astype(BF16)
    for l in loads[2:]:
        l.wait()
    br, bc = mask_ref.shape
    bs = dr // br
    for i in range(br):
        row = lax.rem(c * (br // 2) + i, br)
        for j in range(bc):
            sl = (pl.ds(i * bs, bs), pl.ds(j * bs, bs))
            keep = jnp.full((bs, bs), mask_ref[row, j], jnp.int32) > 0
            wm[sl] = jnp.where(keep, wm[sl], jnp.zeros((bs, bs), BF16))
    pl.semaphore_wait(bar, nz + nq - 1)

    def steps_of(d, u):
        return half if (u < SUB // 2) == (d == 0) else half - 1

    pairs = [(d, u, 1 - 2 * d, steps_of(d, u)) for u in range(SUB) for d in range(2)]

    def sub(u):
        return pl.ds(u * rsub, rsub)

    def held(d, s):
        return s * 2 - 1 + d

    def ag(d, u, sg, s, src=None, dst=None):
        src = held(d, s) if src is None else src
        dst = held(d, s + 1) if dst is None else dst
        return remote(hall.at[src, sub(u)], hall.at[dst, sub(u)], ag_s, ag_r.at[d, u, s], zdev(sg))

    def y_send(i, k):
        remote(ysend.at[pl.ds(i, k)], yprt.at[pl.ds(i, k)], yp_s, yp_r.at[i], pdev).start()

    def y_dot(i, k):
        v = nt_dot(hall[pl.ds(i, k)].reshape(k * tok, ffc), wm[...])
        ysend[pl.ds(i, k)] = v[:, dw_h:].astype(BF16).reshape(k, tok, dw_h)
        yown[pl.ds(i, k)] = v[:, :dw_h].reshape(k, tok, dw_h)
        y_send(i, k)

    def y_add(i, k):
        rows = pl.ds(i, k)
        drain(yprt.at[rows], yp_r.at[i])
        ysum[rows] = (yown[rows] + yprt[rows].astype(F32)).astype(BF16)

    def y_scatter(n):
        lo, hi = grps[n]
        rows = pl.ds(lo, hi - lo)
        local(ysum.at[(rows,) + tile(p)], yrecv.at[p, rows], yr_r.at[n]).start()

        @pl.loop(1, nq)
        def _(k):
            q = qmod(p + k)
            remote(ysum.at[(rows,) + tile(q)], yrecv.at[p, rows], yr_s, yr_r.at[n], qdev(q)).start()

    def y_finish(n):
        lo, hi = grps[n]
        rows = pl.ds(lo, hi - lo)
        drain(yrecv.at[:, rows], yr_r.at[n])
        osum[rows] = jnp.sum(yrecv[:, rows].astype(F32), axis=0).astype(BF16)
        for i in range(lo, hi):
            if i == 0:
                local(osum.at[0], oB.at[z], oB_r).start()
            else:
                off = -((i + 1) // 2) if i % 2 else i // 2
                remote(osum.at[i], oB.at[z], oB_s, oB_r, zdev(off)).start()

    def cot_one():
        local(cot_v.at[tile(p)], cA.at[p], cA_r).start()

        @pl.loop(1, nq)
        def _(k):
            q = qmod(p + k)
            remote(cot_v.at[tile(q)], cA.at[p], cA_s, cA_r, qdev(q)).start()

    near = nz // 2

    def cot_two():
        drain(cA, cA_r)
        local(cA.at[z], cB.at[0], cB_r.at[0]).start()

        def to(k, idx):
            dev = zdev(k)
            remote(cA.at[dev[0]], cB.at[idx], cB_s, cB_r.at[lax.div(idx, near)], dev).start()

        @pl.loop(1, half)
        def _(m):
            to(m, 2 * m - 1)
            to(-m, 2 * m)

        dev = zdev(half)
        remote(cA.at[dev[0]], cB.at[nz - 1], cB_s, cB_r.at[1], dev).start()

    def cot_three(n):
        rows = pl.ds(n * near, near)
        drain(cB.at[rows], cB_r.at[n])
        dst = call.at[(rows,) + tile(p)]
        local(cB.at[rows], dst, cg_r.at[n]).start()

        @pl.loop(1, nq)
        def _(k):
            remote(cB.at[rows], dst, cg_s, cg_r.at[n], qdev(qmod(p + k))).start()

    def cot_pass(n):
        rows = pl.ds(n * near, near)
        ref = call.at[rows, :, pl.ds(0, dw_h)]
        drain(ref, cg_r.at[n])
        remote(ref, call.at[rows, :, pl.ds(dw_h, dw_h)], rel_s, rel_r.at[n], pdev).start()

    def cot_have(n):
        drain(call.at[pl.ds(n * near, near), :, pl.ds(dw_h, dw_h)], rel_r.at[n])

    for d, u, sg, n in pairs:
        ag(d, u, sg, 0, src=0).start()
    cot_one()
    y_dot(0, 1)

    def ag_step(s, u_static, events):
        for d, u, sg, n in pairs:
            drain(hall.at[held(d, s), sub(u)], ag_r.at[d, u, s - 1])
            if u_static is None:
                ag(d, u, sg, s).start()
            elif n == half:
                ag(d, u, sg, s, dst=nz - 1).start()
            if u == SUB // 2 - 1 and d == 1:
                if u_static is not None and half == 2:
                    y_add(0, 1)
                elif u_static is not None:
                    y_add(2 * s - 3, 2)
                else:
                    @pl.when(s == 1)
                    def _():
                        y_add(0, 1)

                    @pl.when(s > 1)
                    def _():
                        y_add(2 * s - 3, 2)
                for at, fn in events:
                    if u_static is None:
                        pl.when(s == at)(fn)
                    elif at >= u_static:
                        fn()
        y_dot(2 * s - 1, 2)

    if big:
        events = [(2, cot_two), (4, functools.partial(cot_three, 0)), (5, functools.partial(cot_three, 1)),
                  (5, functools.partial(y_scatter, 0)), (6, functools.partial(y_scatter, 1)),
                  (7, functools.partial(cot_pass, 0))]
    else:
        events = [(7, cot_two), (7, functools.partial(cot_three, 0)), (7, functools.partial(cot_three, 1)),
                  (7, functools.partial(cot_pass, 0))]

    @pl.loop(1, half - 1)
    def _(s):
        ag_step(s, None, events)

    ag_step(half - 1, half - 1, events)
    cot_pass(1)
    for d, u, sg, n in pairs:
        if n == half:
            drain(hall.at[nz - 1, sub(u)], ag_r.at[d, u, half - 1])
    y_dot(nz - 1, 1)
    y_add(nz - 3, 2)
    cot_have(0)
    cot_have(1)

    def rs(d, u, sg, s):
        return remote(sbuf.at[d, s, sub(u)], rbuf.at[d, s, sub(u)], rs_s, rs_r.at[d, u, s], zdev(sg))

    def part(s, buf):
        m = half - s
        v = jnp.dot(call[pl.ds(2 * m - 1, 2)].reshape(2 * tok, dr), wm[...], preferred_element_type=F32)
        pbuf[buf] = v.reshape(2, tok, ffc)

    def part_one(i):
        pbuf[0, 0] = jnp.dot(call[i], wm[...], preferred_element_type=F32)

    def dw(n):
        lo, hi = n * nz // 4, (n + 1) * nz // 4
        v = tn_dot(call[lo:hi].reshape((hi - lo) * tok, dr), hall[lo:hi].reshape((hi - lo) * tok, ffc))
        if n == 0:
            acc[...] = v
        elif n < 3:
            acc[...] += v
        else:
            accb[...] = (acc[...] + v).astype(BF16)
            local(accb.at[pl.ds(0, dw_h)], dw_hbm.at[pl.ds(mine, dw_h)], st.at[0]).start()
            local(accb.at[pl.ds(dw_h, dw_h)], dw_hbm.at[pl.ds(other, dw_h)], st.at[1]).start()

    part_one(nz - 1)
    for d, u, sg, n in pairs:
        if n == half:
            sbuf[d, 0, sub(u)] = pbuf[0, 0, sub(u)].astype(BF16)
    for d, u, sg, n in pairs:
        if n == half:
            rs(d, u, sg, 0).start()
    part(1, 1)
    for d, u, sg, n in pairs:
        if n < half:
            sbuf[d, 1, sub(u)] = pbuf[1, 1 - d, sub(u)].astype(BF16)
    for d, u, sg, n in pairs:
        if n < half:
            rs(d, u, sg, 1).start()
    y_add(nz - 1, 1)
    for n in range(2 if big else 0, len(grps)):
        y_scatter(n)
    dw(0)

    def out_two():
        drain(oB, oB_r)
        local(oB.at[p], out_v.at[tile(p)], ov_r).start()

        @pl.loop(1, nq)
        def _(k):
            q = qmod(p + k)
            remote(oB.at[q], out_v.at[tile(p)], ov_s, ov_r, qdev(q)).start()

    if big:
        mids = [(1, functools.partial(dw, 1)), (2, functools.partial(dw, 2)), (3, functools.partial(dw, 3)),
                (2, functools.partial(y_finish, 0)), (3, functools.partial(y_finish, 1)),
                (4, functools.partial(y_finish, 2)), (4, functools.partial(y_finish, 3)), (7, out_two)]
    else:
        mids = [(1, functools.partial(dw, n)) for n in (1, 2, 3)]
        mids += [(1, functools.partial(y_finish, n)) for n in range(len(grps))] + [(1, out_two)]

    def rs_add(d, u, s):
        drain(rbuf.at[d, s - 1, sub(u)], rs_r.at[d, u, s - 1])
        sbuf[d, s, sub(u)] = (pbuf[lax.rem(s, 2), 1 - d, sub(u)]
                              + rbuf[d, s - 1, sub(u)].astype(F32)).astype(BF16)

    @pl.loop(1, half)
    def _(s):
        for d, u, sg, n in pairs:
            if n == half:
                rs_add(d, u, s)
                rs(d, u, sg, s).start()
            else:
                @pl.when(s > 1)
                def _():
                    rs_add(d, u, s)
                    rs(d, u, sg, s).start()
            if u == SUB // 2 - 1 and d == 1:
                @pl.when(s < half - 1)
                def _():
                    part(s + 1, lax.rem(s + 1, 2))
        for at, fn in mids:
            pl.when(s == at)(fn)

    part_one(0)
    for d, u, sg, n in pairs:
        drain(rbuf.at[d, half - 1, sub(u)], rs_r.at[d, u, half - 1])
        if d == 1:
            pbuf[0, 0, sub(u)] += (rbuf[0, half - 1, sub(u)].astype(F32)
                                   + rbuf[1, half - 1, sub(u)].astype(F32))
    local(pbuf.at[0, 0], dh_hbm, st.at[2]).start()
    drain(out_v, ov_r)
    local(out_v, out_hbm, st.at[3]).start()

    most = pl.ds(0, nz - 1)
    rest = pl.ds(0, nq - 1)
    drain(hall.at[most], ag_s)
    drain(hall.at[most], rs_s)
    drain(cA.at[rest], cA_s)
    drain(cB.at[most], cB_s)
    drain(call.at[rest, :, pl.ds(0, dw_h)], cg_s)
    drain(call.at[:, :, pl.ds(0, dw_h)], rel_s)
    drain(ysend, yp_s)
    drain(yrecv.at[rest], yr_s)
    drain(oB.at[most], oB_s)
    drain(oB.at[rest], ov_s)
    drain(accb.at[pl.ds(0, dw_h)], st.at[0])
    drain(accb.at[pl.ds(0, dw_h)], st.at[1])
    local(pbuf.at[0, 0], dh_hbm, st.at[2]).wait()
    local(out_v, out_hbm, st.at[3]).wait()


def finish(gate_ref, up_ref, mask_ref, outr_ref, dh_ref, dw_ref, out_ref, dgate_ref, dup_ref, ddown_ref):
    tok = gate_ref.shape[0]
    for r in range(0, tok, 32):
        rows = pl.ds(r, 32)
        dh = dh_ref[rows, :]
        g = gate_ref[rows, :].astype(F32)
        sig = 1.0 / (1.0 + jnp.exp(-g))
        dgate_ref[rows, :] = (dh * up_ref[rows, :].astype(F32) * sig * (1.0 + g * (1.0 - sig))).astype(BF16)
        dup_ref[rows, :] = (dh * (g * sig)).astype(BF16)
    br, bc = mask_ref.shape
    bs = dw_ref.shape[0] // br
    for i in range(br):
        for j in range(bc):
            sl = (pl.ds(i * bs, bs), pl.ds(j * bs, bs))
            keep = jnp.full((bs, bs), mask_ref[i, j], jnp.int32) > 0
            ddown_ref[sl] = jnp.where(keep, dw_ref[sl], jnp.zeros((bs, bs), BF16))
    out_ref[...] = outr_ref[...]


def body(nz, nq, gate_pre, up_pre, down_weight, block_mask, cotangent):
    tok, ffc = gate_pre.shape
    dr = down_weight.shape[0]
    dw_h = dr // 2
    half = nz // 2
    ng = len(groups(nz))
    dma = pltpu.SemaphoreType.DMA
    vm = pltpu.VMEM
    any_ = pl.BlockSpec(memory_space=pl.ANY)
    vmem = pl.BlockSpec(memory_space=pltpu.VMEM)
    smem = pl.BlockSpec(memory_space=pltpu.SMEM)
    outr, dh, dwr = pl.pallas_call(
        functools.partial(kernel, nz, nq),
        out_shape=(
            jax.ShapeDtypeStruct((tok, dw_h), BF16),
            jax.ShapeDtypeStruct((tok, ffc), F32),
            jax.ShapeDtypeStruct((dr, ffc), BF16),
        ),
        in_specs=[any_, any_, any_, smem, any_],
        out_specs=(any_,) * 3,
        scratch_shapes=[
            vm((tok, ffc), BF16), vm((tok, ffc), BF16), vm((dr, ffc), BF16), vm((tok, dw_h), BF16),
            vm((nz, tok, ffc), BF16), vm((nz, tok, dr), BF16),
            vm((nq, TR, TC), BF16), vm((nz, TR, TC), BF16),
            vm((nz, tok, dw_h), F32), vm((nz, tok, dw_h), BF16), vm((nz, tok, dw_h), BF16),
            vm((nz, tok, dw_h), BF16), vm((nq, nz, TR, TC), BF16),
            vm((nz, TR, TC), BF16), vm((nz, TR, TC), BF16), vm((tok, dw_h), BF16),
            vm((2, half, tok, ffc), BF16), vm((2, half, tok, ffc), BF16),
            vm((2, 2, tok, ffc), F32), vm((dr, ffc), F32), vm((dr, ffc), BF16),
            dma((5,)), dma, dma((2, SUB, half)), dma, dma((2, SUB, half)),
            dma, dma, dma, dma((2,)),
            dma, dma((2,)), dma, dma((2,)), dma, dma((nz,)), dma, dma((ng,)),
            dma, dma, dma, dma, dma((4,)),
        ],
        compiler_params=pltpu.CompilerParams(
            collective_id=0, has_side_effects=True, vmem_limit_bytes=60 * 1024 * 1024),
    )(gate_pre, up_pre, down_weight, block_mask, cotangent)
    return pl.pallas_call(
        finish,
        out_shape=(
            jax.ShapeDtypeStruct((tok, dw_h), BF16),
            jax.ShapeDtypeStruct((tok, ffc), BF16),
            jax.ShapeDtypeStruct((tok, ffc), BF16),
            jax.ShapeDtypeStruct((dr, ffc), BF16),
        ),
        in_specs=[vmem, vmem, smem, vmem, vmem, vmem],
        out_specs=(vmem,) * 4,
    )(gate_pre, up_pre, block_mask, outr, dh, dwr)


def solution(mesh):
    nz = mesh.shape["row"]
    nq = mesh.shape["col"] // 2
    spec = P("row", "col")
    return jax.shard_map(functools.partial(body, nz, nq), mesh=mesh, in_specs=(spec,) * 5,
                         out_specs=(spec,) * 4, check_vma=False)
```

```python
import functools

import jax
import jax.numpy as jnp
from jax import lax
from jax.experimental import pallas as pl
from jax.experimental.pallas import tpu as pltpu
from jax.sharding import PartitionSpec as P

MESH = pl.DeviceIdType.MESH
SUB = 4
TR = 16
TC = 128
F32 = jnp.float32
BF16 = jnp.bfloat16


def nt_dot(a, b):
    return lax.dot_general(a, b, (((1,), (1,)), ((), ())), preferred_element_type=F32)


def tn_dot(a, b):
    return lax.dot_general(a, b, (((0,), (0,)), ((), ())), preferred_element_type=F32)


def groups(nz):
    half = nz // 2
    if half <= 4:
        return [(i, i + 1) for i in range(nz)]
    cut = [0, half - 3, nz - 5, nz]
    return list(zip(cut[:-1], cut[1:]))


def cot_groups(nz):
    half = nz // 2
    if half <= 4:
        return [(0, 1), (1, 2), (2, nz)]
    return [(0, half - 1), (half - 1, nz - 3), (nz - 3, nz)]


def kernel(nz, nq, gate_hbm, up_hbm, w_hbm, mask_ref, cot_hbm,
           out_hbm, dh_hbm, dw_hbm,
           gate_v, up_v, wm, cot_v, hall, call, cA, cB,
           yown, ysend, yprt, ysum, yrecv, osum, oB, out_v,
           rbuf, sbuf, pbuf, acc, accb,
           ld, ag_s, ag_r, rs_s, rs_r, cA_s, cA_r, cB_s, cB_r,
           cg_s, cg_r, rel_s, rel_r, yp_s, yp_r, yr_s, yr_r,
           oB_s, oB_r, ov_s, ov_r, st):
    z = lax.axis_index("row")
    col = lax.axis_index("col")
    p = lax.div(col, 2)
    c = lax.rem(col, 2)
    half = nz // 2
    tok, ffc = gate_v.shape
    dr = wm.shape[0]
    dw_h = dr // 2
    rsub = tok // SUB
    big = half > 4
    grps = groups(nz)
    cgrps = cot_groups(nz)

    def zdev(k):
        return (lax.rem(z + (k + nz), nz), col)

    def qmod(v):
        return lax.rem(v + nq, nq)

    def tile(q):
        return (pl.ds(pl.multiple_of(lax.div(q, 2) * TR, TR), TR),
                pl.ds(pl.multiple_of(lax.rem(q, 2) * TC, TC), TC))

    def qdev(q):
        return (z, q * 2 + c)

    pdev = (z, p * 2 + (1 - c))
    mine = pl.multiple_of(c * dw_h, TC)
    other = pl.multiple_of((1 - c) * dw_h, TC)

    def remote(src, dst, ss, rs, dev):
        return pltpu.make_async_remote_copy(
            src_ref=src, dst_ref=dst, send_sem=ss, recv_sem=rs,
            device_id=dev, device_id_type=MESH)

    def local(src, dst, sem):
        return pltpu.make_async_copy(src, dst, sem)

    def drain(ref, sem):
        pltpu.make_async_copy(ref, ref, sem).wait()

    bar = pltpu.get_barrier_semaphore()

    @pl.loop(1, nz)
    def _(k):
        pl.semaphore_signal(bar, inc=1, device_id=zdev(k), device_id_type=MESH)

    @pl.loop(1, nq)
    def _(k):
        pl.semaphore_signal(bar, inc=1, device_id=qdev(qmod(p + k)), device_id_type=MESH)

    pl.semaphore_signal(bar, inc=1, device_id=pdev, device_id_type=MESH)

    loads = [local(a, b, ld.at[i]) for i, (a, b) in enumerate((
        (gate_hbm, gate_v), (up_hbm, up_v), (cot_hbm, cot_v),
        (w_hbm.at[pl.ds(mine, dw_h)], wm.at[pl.ds(0, dw_h)]),
        (w_hbm.at[pl.ds(other, dw_h)], wm.at[pl.ds(dw_h, dw_h)])))]
    for l in loads:
        l.start()
    loads[0].wait()
    loads[1].wait()
    g = gate_v[...].astype(F32)
    hall[0] = (g / (1.0 + jnp.exp(-g)) * up_v[...].astype(F32)).astype(BF16)
    for l in loads[2:]:
        l.wait()
    br, bc = mask_ref.shape
    bs = dr // br
    for i in range(br):
        row = lax.rem(c * (br // 2) + i, br)
        for j in range(bc):
            sl = (pl.ds(i * bs, bs), pl.ds(j * bs, bs))
            keep = jnp.full((bs, bs), mask_ref[row, j], jnp.int32) > 0
            wm[sl] = jnp.where(keep, wm[sl], jnp.zeros((bs, bs), BF16))
    pl.semaphore_wait(bar, nz + nq - 1)

    def steps_of(d, u):
        return half if (u < SUB // 2) == (d == 0) else half - 1

    pairs = [(d, u, 1 - 2 * d, steps_of(d, u)) for u in range(SUB) for d in range(2)]

    def sub(u):
        return pl.ds(u * rsub, rsub)

    def held(d, s):
        return s * 2 - 1 + d

    def ag(d, u, sg, s, src=None, dst=None):
        src = held(d, s) if src is None else src
        dst = held(d, s + 1) if dst is None else dst
        return remote(hall.at[src, sub(u)], hall.at[dst, sub(u)], ag_s, ag_r.at[d, u, s], zdev(sg))

    def y_send(i, k):
        remote(ysend.at[pl.ds(i, k)], yprt.at[pl.ds(i, k)], yp_s, yp_r.at[i], pdev).start()

    def y_dot(i, k):
        v = nt_dot(hall[pl.ds(i, k)].reshape(k * tok, ffc), wm[...])
        ysend[pl.ds(i, k)] = v[:, dw_h:].astype(BF16).reshape(k, tok, dw_h)
        yown[pl.ds(i, k)] = v[:, :dw_h].reshape(k, tok, dw_h)
        y_send(i, k)

    def y_add(i, k):
        rows = pl.ds(i, k)
        drain(yprt.at[rows], yp_r.at[i])
        ysum[rows] = (yown[rows] + yprt[rows].astype(F32)).astype(BF16)

    def y_scatter(n):
        lo, hi = grps[n]
        rows = pl.ds(lo, hi - lo)
        local(ysum.at[(rows,) + tile(p)], yrecv.at[p, rows], yr_r.at[n]).start()

        @pl.loop(1, nq)
        def _(k):
            q = qmod(p + k)
            remote(ysum.at[(rows,) + tile(q)], yrecv.at[p, rows], yr_s, yr_r.at[n], qdev(q)).start()

    def y_finish(n):
        lo, hi = grps[n]
        rows = pl.ds(lo, hi - lo)
        drain(yrecv.at[:, rows], yr_r.at[n])
        osum[rows] = jnp.sum(yrecv[:, rows].astype(F32), axis=0).astype(BF16)
        for i in range(lo, hi):
            if i == 0:
                local(osum.at[0], oB.at[z], oB_r).start()
            else:
                off = -((i + 1) // 2) if i % 2 else i // 2
                remote(osum.at[i], oB.at[z], oB_s, oB_r, zdev(off)).start()

    def cot_one():
        local(cot_v.at[tile(p)], cA.at[p], cA_r).start()

        @pl.loop(1, nq)
        def _(k):
            q = qmod(p + k)
            remote(cot_v.at[tile(q)], cA.at[p], cA_s, cA_r, qdev(q)).start()

    def crows(n):
        return pl.ds(cgrps[n][0], cgrps[n][1] - cgrps[n][0])

    def cot_two():
        drain(cA, cA_r)
        local(cA.at[z], cB.at[0], cB_r.at[0]).start()
        for i in range(nz - 1, 0, -1):
            k = (i + 1) // 2 if i % 2 else -(i // 2)
            n = [lo <= i < hi for lo, hi in cgrps].index(True)
            dev = zdev(k)
            remote(cA.at[dev[0]], cB.at[i], cB_s, cB_r.at[n], dev).start()

    def cot_three(n):
        rows = crows(n)
        drain(cB.at[rows], cB_r.at[n])
        dst = call.at[(rows,) + tile(p)]
        local(cB.at[rows], dst, cg_r.at[n]).start()

        @pl.loop(1, nq)
        def _(k):
            remote(cB.at[rows], dst, cg_s, cg_r.at[n], qdev(qmod(p + k))).start()

    def cot_pass(n):
        ref = call.at[crows(n), :, pl.ds(0, dw_h)]
        drain(ref, cg_r.at[n])
        remote(ref, call.at[crows(n), :, pl.ds(dw_h, dw_h)], rel_s, rel_r.at[n], pdev).start()

    def cot_have(n):
        drain(call.at[crows(n), :, pl.ds(dw_h, dw_h)], rel_r.at[n])

    def ag_far(d, u, sg, src):
        remote(hall.at[src, sub(u)], hall.at[nz - 1, sub(u)], ag_s, ag_r.at[d, u, half - 1], zdev(2 * sg)).start()

    cot_one()
    for d, u, sg, n in pairs:
        ag(d, u, sg, 0, src=0).start()
        if half == 2 and n == half:
            ag_far(d, u, sg, 0)
    y_dot(0, 1)

    near, mid, far = 0, 1, 2
    events = [(1, cot_two), (3, functools.partial(cot_three, near)), (4, functools.partial(cot_three, far)),
              (4, functools.partial(cot_three, mid)), (5, functools.partial(y_scatter, 0)),
              (6, functools.partial(cot_pass, near)), (6, functools.partial(cot_pass, far))]

    @pl.loop(1, half - 1)
    def _(s):
        for d, u, sg, n in pairs:
            drain(hall.at[held(d, s), sub(u)], ag_r.at[d, u, s - 1])
            ag(d, u, sg, s).start()
            if n == half:
                @pl.when(s == half - 2)
                def _():
                    ag_far(d, u, sg, held(d, s))
            if u == 0 and d == 1:
                @pl.when(s == 1)
                def _():
                    y_add(0, 1)

                @pl.when(s > 1)
                def _():
                    y_add(2 * s - 3, 2)
        y_dot(2 * s - 1, 2)
        for at, fn in events:
            pl.when(s == at)(fn)

    if not big:
        for at, fn in events:
            if fn is not events[4][1]:
                fn()
    for d, u, sg, n in pairs:
        drain(hall.at[held(d, half - 1), sub(u)], ag_r.at[d, u, half - 2])
    cot_have(far)

    def rs(d, u, sg, s):
        return remote(sbuf.at[d, s, sub(u)], rbuf.at[d, s, sub(u)], rs_s, rs_r.at[d, u, s], zdev(sg))

    def part(s, buf):
        m = half - s
        v = jnp.dot(call[pl.ds(2 * m - 1, 2)].reshape(2 * tok, dr), wm[...], preferred_element_type=F32)
        pbuf[buf] = v.reshape(2, tok, ffc)

    def part_one(i):
        pbuf[0, 0] = jnp.dot(call[i], wm[...], preferred_element_type=F32)

    def dw(n):
        lo, hi = n * nz // 4, (n + 1) * nz // 4
        v = tn_dot(call[lo:hi].reshape((hi - lo) * tok, dr), hall[lo:hi].reshape((hi - lo) * tok, ffc))
        if n == 0:
            acc[...] = v
        elif n < 3:
            acc[...] += v
        else:
            accb[...] = (acc[...] + v).astype(BF16)
            local(accb.at[pl.ds(0, dw_h)], dw_hbm.at[pl.ds(mine, dw_h)], st.at[0]).start()
            local(accb.at[pl.ds(dw_h, dw_h)], dw_hbm.at[pl.ds(other, dw_h)], st.at[1]).start()

    if not big:
        cot_pass(mid)
        cot_have(mid)
        cot_have(near)
    part_one(nz - 1)
    for d, u, sg, n in pairs:
        if n == half:
            sbuf[d, 0, sub(u)] = pbuf[0, 0, sub(u)].astype(BF16)
            remote(sbuf.at[d, 0, sub(u)], rbuf.at[d, 0, sub(u)], rs_s, rs_r.at[d, u, 0], zdev(2 * sg)).start()
    part(1, 1)
    for d, u, sg, n in pairs:
        sbuf[d, 1, sub(u)] = pbuf[1, 1 - d, sub(u)].astype(BF16)
        rs(d, u, sg, 1).start()
    if big:
        cot_pass(mid)
        y_add(nz - 5, 2)
        y_scatter(1)
        y_dot(nz - 3, 2)
    else:
        y_add(0, 1)
        y_dot(1, 2)
    for d, u, sg, n in pairs:
        if n == half:
            drain(hall.at[nz - 1, sub(u)], ag_r.at[d, u, half - 1])
    y_dot(nz - 1, 1)
    y_add(nz - 3, 2)
    if big:
        cot_have(mid)
        part(2, 0)
    y_add(nz - 1, 1)
    if big:
        y_scatter(2)
        cot_have(near)
    else:
        for n in range(len(grps)):
            y_scatter(n)
        for n in range(4):
            dw(n)

    def out_two():
        drain(oB, oB_r)
        local(oB.at[p], out_v.at[tile(p)], ov_r).start()

        @pl.loop(1, nq)
        def _(k):
            q = qmod(p + k)
            remote(oB.at[q], out_v.at[tile(p)], ov_s, ov_r, qdev(q)).start()

    mids = [(2, functools.partial(y_finish, 0)), (2, functools.partial(y_finish, 1)),
            (3, functools.partial(y_finish, 2)), (4, functools.partial(dw, 0)), (4, functools.partial(dw, 1)),
            (5, functools.partial(dw, 2)), (5, functools.partial(dw, 3)), (6, out_two)]
    if not big:
        for n in range(len(grps)):
            y_finish(n)
        out_two()

    def rs_add(d, u, s):
        drain(rbuf.at[d, s - 1, sub(u)], rs_r.at[d, u, s - 1])
        sbuf[d, s, sub(u)] = (pbuf[lax.rem(s, 2), 1 - d, sub(u)]
                              + rbuf[d, s - 1, sub(u)].astype(F32)).astype(BF16)

    @pl.loop(2, half)
    def _(s):
        for d, u, sg, n in pairs:
            if n == half:
                @pl.when(s == 2)
                def _():
                    drain(rbuf.at[d, 0, sub(u)], rs_r.at[d, u, 0])
                    pbuf[0, 1 - d, sub(u)] += rbuf[d, 0, sub(u)].astype(F32)

            rs_add(d, u, s)
            rs(d, u, sg, s).start()
            if u == SUB // 2 - 1 and d == 1:
                @pl.when(s < half - 1)
                def _():
                    part(s + 1, lax.rem(s + 1, 2))
        for at, fn in mids:
            pl.when(s == at)(fn)

    part_one(0)
    for d, u, sg, n in pairs:
        drain(rbuf.at[d, half - 1, sub(u)], rs_r.at[d, u, half - 1])
        if half == 2 and n == half:
            drain(rbuf.at[d, 0, sub(u)], rs_r.at[d, u, 0])
            pbuf[0, 0, sub(u)] += rbuf[d, 0, sub(u)].astype(F32)
        if d == 1:
            pbuf[0, 0, sub(u)] += (rbuf[0, half - 1, sub(u)].astype(F32)
                                   + rbuf[1, half - 1, sub(u)].astype(F32))
    local(pbuf.at[0, 0], dh_hbm, st.at[2]).start()
    drain(out_v, ov_r)
    local(out_v, out_hbm, st.at[3]).start()

    most = pl.ds(0, nz - 1)
    rest = pl.ds(0, nq - 1)
    drain(hall.at[most], ag_s)
    drain(hall.at[most], rs_s)
    drain(cA.at[rest], cA_s)
    drain(cB.at[most], cB_s)
    drain(call.at[rest, :, pl.ds(0, dw_h)], cg_s)
    drain(call.at[:, :, pl.ds(0, dw_h)], rel_s)
    drain(ysend, yp_s)
    drain(yrecv.at[rest], yr_s)
    drain(oB.at[most], oB_s)
    drain(oB.at[rest], ov_s)
    drain(accb.at[pl.ds(0, dw_h)], st.at[0])
    drain(accb.at[pl.ds(0, dw_h)], st.at[1])
    local(pbuf.at[0, 0], dh_hbm, st.at[2]).wait()
    local(out_v, out_hbm, st.at[3]).wait()


def finish(gate_ref, up_ref, mask_ref, outr_ref, dh_ref, dw_ref, out_ref, dgate_ref, dup_ref, ddown_ref):
    tok = gate_ref.shape[0]
    for r in range(0, tok, 32):
        rows = pl.ds(r, 32)
        dh = dh_ref[rows, :]
        g = gate_ref[rows, :].astype(F32)
        sig = 1.0 / (1.0 + jnp.exp(-g))
        dgate_ref[rows, :] = (dh * up_ref[rows, :].astype(F32) * sig * (1.0 + g * (1.0 - sig))).astype(BF16)
        dup_ref[rows, :] = (dh * (g * sig)).astype(BF16)
    br, bc = mask_ref.shape
    bs = dw_ref.shape[0] // br
    for i in range(br):
        for j in range(bc):
            sl = (pl.ds(i * bs, bs), pl.ds(j * bs, bs))
            keep = jnp.full((bs, bs), mask_ref[i, j], jnp.int32) > 0
            ddown_ref[sl] = jnp.where(keep, dw_ref[sl], jnp.zeros((bs, bs), BF16))
    out_ref[...] = outr_ref[...]


def body(nz, nq, gate_pre, up_pre, down_weight, block_mask, cotangent):
    tok, ffc = gate_pre.shape
    dr = down_weight.shape[0]
    dw_h = dr // 2
    half = nz // 2
    ng = len(groups(nz))
    dma = pltpu.SemaphoreType.DMA
    vm = pltpu.VMEM
    any_ = pl.BlockSpec(memory_space=pl.ANY)
    vmem = pl.BlockSpec(memory_space=pltpu.VMEM)
    smem = pl.BlockSpec(memory_space=pltpu.SMEM)
    outr, dh, dwr = pl.pallas_call(
        functools.partial(kernel, nz, nq),
        out_shape=(
            jax.ShapeDtypeStruct((tok, dw_h), BF16),
            jax.ShapeDtypeStruct((tok, ffc), F32),
            jax.ShapeDtypeStruct((dr, ffc), BF16),
        ),
        in_specs=[any_, any_, any_, smem, any_],
        out_specs=(any_,) * 3,
        scratch_shapes=[
            vm((tok, ffc), BF16), vm((tok, ffc), BF16), vm((dr, ffc), BF16), vm((tok, dw_h), BF16),
            vm((nz, tok, ffc), BF16), vm((nz, tok, dr), BF16),
            vm((nq, TR, TC), BF16), vm((nz, TR, TC), BF16),
            vm((nz, tok, dw_h), F32), vm((nz, tok, dw_h), BF16), vm((nz, tok, dw_h), BF16),
            vm((nz, tok, dw_h), BF16), vm((nq, nz, TR, TC), BF16),
            vm((nz, TR, TC), BF16), vm((nz, TR, TC), BF16), vm((tok, dw_h), BF16),
            vm((2, half, tok, ffc), BF16), vm((2, half, tok, ffc), BF16),
            vm((2, 2, tok, ffc), F32), vm((dr, ffc), F32), vm((dr, ffc), BF16),
            dma((5,)), dma, dma((2, SUB, half)), dma, dma((2, SUB, half)),
            dma, dma, dma, dma((3,)),
            dma, dma((3,)), dma, dma((3,)), dma, dma((nz,)), dma, dma((ng,)),
            dma, dma, dma, dma, dma((4,)),
        ],
        compiler_params=pltpu.CompilerParams(
            collective_id=0, has_side_effects=True, vmem_limit_bytes=60 * 1024 * 1024),
    )(gate_pre, up_pre, down_weight, block_mask, cotangent)
    return pl.pallas_call(
        finish,
        out_shape=(
            jax.ShapeDtypeStruct((tok, dw_h), BF16),
            jax.ShapeDtypeStruct((tok, ffc), BF16),
            jax.ShapeDtypeStruct((tok, ffc), BF16),
            jax.ShapeDtypeStruct((dr, ffc), BF16),
        ),
        in_specs=[vmem, vmem, smem, vmem, vmem, vmem],
        out_specs=(vmem,) * 4,
    )(gate_pre, up_pre, block_mask, outr, dh, dwr)


def solution(mesh):
    nz = mesh.shape["row"]
    nq = mesh.shape["col"] // 2
    spec = P("row", "col")
    return jax.shard_map(functools.partial(body, nz, nq), mesh=mesh, in_specs=(spec,) * 5,
                         out_specs=(spec,) * 4, check_vma=False)
```

```python
import functools

import jax
import jax.numpy as jnp
from jax import lax
from jax.experimental import pallas as pl
from jax.experimental.pallas import tpu as pltpu
from jax.sharding import PartitionSpec as P

MESH = pl.DeviceIdType.MESH
SUB = 4
TR = 16
TC = 128
F32 = jnp.float32
BF16 = jnp.bfloat16


def nt_dot(a, b):
    return lax.dot_general(a, b, (((1,), (1,)), ((), ())), preferred_element_type=F32)


def tn_dot(a, b):
    return lax.dot_general(a, b, (((0,), (0,)), ((), ())), preferred_element_type=F32)


def groups(nz):
    half = nz // 2
    if half <= 4:
        return [(i, i + 1) for i in range(nz)]
    cut = [0, 3, nz - 5, nz]
    return list(zip(cut[:-1], cut[1:]))


def cot_groups(nz):
    half = nz // 2
    if half <= 4:
        return [(0, 1), (1, 2), (2, nz)]
    return [(0, half - 1), (half - 1, nz - 3), (nz - 3, nz)]


def kernel(nz, nq, gate_hbm, up_hbm, w_hbm, mask_ref, cot_hbm,
           out_hbm, dh_hbm, dw_hbm,
           gate_v, up_v, wm, cot_v, hall, call, cA, cB,
           yown, ysend, yprt, ysum, yrecv, osum, oB, out_v,
           rbuf, sbuf, pbuf, acc, accb,
           ld, ag_s, ag_r, rs_s, rs_r, cA_s, cA_r, cB_s, cB_r,
           cg_s, cg_r, rel_s, rel_r, yp_s, yp_r, yr_s, yr_r,
           oB_s, oB_r, ov_s, ov_r, st, far_sem):
    z = lax.axis_index("row")
    col = lax.axis_index("col")
    p = lax.div(col, 2)
    c = lax.rem(col, 2)
    half = nz // 2
    tok, ffc = gate_v.shape
    dr = wm.shape[0]
    dw_h = dr // 2
    rsub = tok // SUB
    big = half > 4
    grps = groups(nz)
    cgrps = cot_groups(nz)

    def zdev(k):
        return (lax.rem(z + (k + nz), nz), col)

    def qmod(v):
        return lax.rem(v + nq, nq)

    def tile(q):
        return (pl.ds(pl.multiple_of(lax.div(q, 2) * TR, TR), TR),
                pl.ds(pl.multiple_of(lax.rem(q, 2) * TC, TC), TC))

    def qdev(q):
        return (z, q * 2 + c)

    pdev = (z, p * 2 + (1 - c))
    mine = pl.multiple_of(c * dw_h, TC)
    other = pl.multiple_of((1 - c) * dw_h, TC)

    def remote(src, dst, ss, rs, dev):
        return pltpu.make_async_remote_copy(
            src_ref=src, dst_ref=dst, send_sem=ss, recv_sem=rs,
            device_id=dev, device_id_type=MESH)

    def local(src, dst, sem):
        return pltpu.make_async_copy(src, dst, sem)

    def drain(ref, sem):
        pltpu.make_async_copy(ref, ref, sem).wait()

    bar = pltpu.get_barrier_semaphore()

    near_z = (1, -1, 2, -2) if big else range(1, nz)
    for k in near_z:
        pl.semaphore_signal(bar, inc=1, device_id=zdev(k), device_id_type=MESH)

    @pl.loop(1, nq)
    def _(k):
        pl.semaphore_signal(bar, inc=1, device_id=qdev(qmod(p + k)), device_id_type=MESH)

    pl.semaphore_signal(bar, inc=1, device_id=pdev, device_id_type=MESH)

    loads = [local(a, b, ld.at[i]) for i, (a, b) in enumerate((
        (gate_hbm, gate_v), (up_hbm, up_v), (cot_hbm, cot_v),
        (w_hbm.at[pl.ds(mine, dw_h)], wm.at[pl.ds(0, dw_h)]),
        (w_hbm.at[pl.ds(other, dw_h)], wm.at[pl.ds(dw_h, dw_h)])))]
    for l in loads:
        l.start()
    loads[0].wait()
    loads[1].wait()
    g = gate_v[...].astype(F32)
    hall[0] = (g / (1.0 + jnp.exp(-g)) * up_v[...].astype(F32)).astype(BF16)
    for l in loads[2:]:
        l.wait()
    br, bc = mask_ref.shape
    bs = dr // br
    for i in range(br):
        row = lax.rem(c * (br // 2) + i, br)
        for j in range(bc):
            sl = (pl.ds(i * bs, bs), pl.ds(j * bs, bs))
            keep = jnp.full((bs, bs), mask_ref[row, j], jnp.int32) > 0
            wm[sl] = jnp.where(keep, wm[sl], jnp.zeros((bs, bs), BF16))
    pl.semaphore_wait(bar, len(near_z) + nq)

    def tell(n):
        for k in (2 << n, -(2 << n)):
            pl.semaphore_signal(far_sem.at[n], inc=1, device_id=zdev(k), device_id_type=MESH)

    def hear(n):
        pl.semaphore_wait(far_sem.at[n], 2)

    if big:
        tell(0)

    def steps_of(d, u):
        return half if (u < SUB // 2) == (d == 0) else half - 1

    pairs = [(d, u, 1 - 2 * d, steps_of(d, u)) for u in range(SUB) for d in range(2)]

    def sub(u):
        return pl.ds(u * rsub, rsub)

    def held(d, s):
        return s * 2 - 1 + d

    def ag(d, u, sg, s, src=None, dst=None):
        src = held(d, s) if src is None else src
        dst = held(d, s + 1) if dst is None else dst
        return remote(hall.at[src, sub(u)], hall.at[dst, sub(u)], ag_s, ag_r.at[d, u, s], zdev(sg))

    def y_send(i, k):
        remote(ysend.at[pl.ds(i, k)], yprt.at[pl.ds(i, k)], yp_s, yp_r.at[i], pdev).start()

    def y_dot(i, k):
        v = nt_dot(hall[pl.ds(i, k)].reshape(k * tok, ffc), wm[...])
        ysend[pl.ds(i, k)] = v[:, dw_h:].astype(BF16).reshape(k, tok, dw_h)
        yown[pl.ds(i, k)] = v[:, :dw_h].reshape(k, tok, dw_h)
        y_send(i, k)

    def y_add(i, k):
        rows = pl.ds(i, k)
        drain(yprt.at[rows], yp_r.at[i])
        ysum[rows] = (yown[rows] + yprt[rows].astype(F32)).astype(BF16)

    def y_scatter(n, first=1, end=nq):
        lo, hi = grps[n]
        rows = pl.ds(lo, hi - lo)
        if first == 1:
            local(ysum.at[(rows,) + tile(p)], yrecv.at[p, rows], yr_r.at[n]).start()

        @pl.loop(first, end)
        def _(k):
            q = qmod(p + k)
            remote(ysum.at[(rows,) + tile(q)], yrecv.at[p, rows], yr_s, yr_r.at[n], qdev(q)).start()

    def y_finish(n):
        lo, hi = grps[n]
        rows = pl.ds(lo, hi - lo)
        drain(yrecv.at[:, rows], yr_r.at[n])
        osum[rows] = jnp.sum(yrecv[:, rows].astype(F32), axis=0).astype(BF16)
        for i in range(lo, hi):
            if i == 0:
                local(osum.at[0], oB.at[z], oB_r).start()
            else:
                off = -((i + 1) // 2) if i % 2 else i // 2
                remote(osum.at[i], oB.at[z], oB_s, oB_r, zdev(off)).start()

    def cot_one():
        local(cot_v.at[tile(p)], cA.at[p], cA_r).start()

        @pl.loop(1, nq)
        def _(k):
            q = qmod(p + k)
            remote(cot_v.at[tile(q)], cA.at[p], cA_s, cA_r, qdev(q)).start()

    def crows(n):
        return pl.ds(cgrps[n][0], cgrps[n][1] - cgrps[n][0])

    def cot_two():
        if big:
            hear(1)
        drain(cA, cA_r)
        local(cA.at[z], cB.at[0], cB_r.at[0]).start()
        for i in range(nz - 1, 0, -1):
            k = (i + 1) // 2 if i % 2 else -(i // 2)
            n = [lo <= i < hi for lo, hi in cgrps].index(True)
            dev = zdev(k)
            remote(cA.at[dev[0]], cB.at[i], cB_s, cB_r.at[n], dev).start()

    def cot_three(n, lo=1, hi=nq):
        rows = crows(n)
        dst = call.at[(rows,) + tile(p)]
        if lo == 1:
            drain(cB.at[rows], cB_r.at[n])
            local(cB.at[rows], dst, cg_r.at[n]).start()

        @pl.loop(lo, hi)
        def _(k):
            remote(cB.at[rows], dst, cg_s, cg_r.at[n], qdev(qmod(p + k))).start()

    def cot_pass(n):
        ref = call.at[crows(n), :, pl.ds(0, dw_h)]
        drain(ref, cg_r.at[n])
        remote(ref, call.at[crows(n), :, pl.ds(dw_h, dw_h)], rel_s, rel_r.at[n], pdev).start()

    def cot_have(n):
        drain(call.at[crows(n), :, pl.ds(dw_h, dw_h)], rel_r.at[n])

    def ag_far(d, u, sg, src):
        remote(hall.at[src, sub(u)], hall.at[nz - 1, sub(u)], ag_s, ag_r.at[d, u, half - 1], zdev(2 * sg)).start()

    cot_one()
    for d, u, sg, n in pairs:
        ag(d, u, sg, 0, src=0).start()
        if half == 2 and n == half:
            ag_far(d, u, sg, 0)
    if big:
        hear(0)
        tell(1)
    y_dot(0, 1)

    near, mid, far = 0, 1, 2
    last = SUB - 1
    cut = nq // 2
    events = [(1, last, cot_two), (2, last, functools.partial(y_scatter, 0)),
              (3, last, functools.partial(cot_three, near)),
              (4, last, functools.partial(cot_three, far)),
              (5, SUB // 4, functools.partial(cot_three, mid, 1, cut)),
              (5, SUB // 2, functools.partial(cot_three, mid, cut, nq)),
              (6, SUB // 4, functools.partial(y_scatter, 1, 1, cut)),
              (6, SUB // 2, functools.partial(y_scatter, 1, cut, nq)),
              (6, last, functools.partial(cot_pass, near)), (6, last, functools.partial(cot_pass, far))]

    @pl.loop(1, half - 1)
    def _(s):
        for d, u, sg, n in pairs:
            drain(hall.at[held(d, s), sub(u)], ag_r.at[d, u, s - 1])
            ag(d, u, sg, s).start()
            if n == half:
                @pl.when(s == half - 2)
                def _():
                    ag_far(d, u, sg, held(d, s))
            if u == 0 and d == 1:
                @pl.when(s == 1)
                def _():
                    y_add(0, 1)

                @pl.when(s > 1)
                def _():
                    y_add(2 * s - 3, 2)
            if d == 1:
                if u == last:
                    y_dot(2 * s - 1, 2)
                for at, on, fn in events:
                    if on == u:
                        pl.when(s == at)(fn)

    if not big:
        for at, on, fn in events:
            if getattr(fn, 'func', None) is not y_scatter:
                fn()
    for d, u, sg, n in pairs:
        drain(hall.at[held(d, half - 1), sub(u)], ag_r.at[d, u, half - 2])
    cot_have(far)

    def rs(d, u, sg, s):
        return remote(sbuf.at[d, s, sub(u)], rbuf.at[d, s, sub(u)], rs_s, rs_r.at[d, u, s], zdev(sg))

    def part(s, buf):
        m = half - s
        v = jnp.dot(call[pl.ds(2 * m - 1, 2)].reshape(2 * tok, dr), wm[...], preferred_element_type=F32)
        pbuf[buf] = v.reshape(2, tok, ffc)

    def part_one(i):
        pbuf[0, 0] = jnp.dot(call[i], wm[...], preferred_element_type=F32)

    def dw(n):
        lo, hi = n * nz // 4, (n + 1) * nz // 4
        v = tn_dot(call[lo:hi].reshape((hi - lo) * tok, dr), hall[lo:hi].reshape((hi - lo) * tok, ffc))
        if n == 0:
            acc[...] = v
        elif n < 3:
            acc[...] += v
        else:
            accb[...] = (acc[...] + v).astype(BF16)
            local(accb.at[pl.ds(0, dw_h)], dw_hbm.at[pl.ds(mine, dw_h)], st.at[0]).start()
            local(accb.at[pl.ds(dw_h, dw_h)], dw_hbm.at[pl.ds(other, dw_h)], st.at[1]).start()

    if not big:
        cot_pass(mid)
        cot_have(mid)
        cot_have(near)
    part_one(nz - 1)
    for d, u, sg, n in pairs:
        if n == half:
            sbuf[d, 0, sub(u)] = pbuf[0, 0, sub(u)].astype(BF16)
            remote(sbuf.at[d, 0, sub(u)], rbuf.at[d, 0, sub(u)], rs_s, rs_r.at[d, u, 0], zdev(2 * sg)).start()
    part(1, 1)
    for d, u, sg, n in pairs:
        sbuf[d, 1, sub(u)] = pbuf[1, 1 - d, sub(u)].astype(BF16)
        rs(d, u, sg, 1).start()
    if big:
        cot_pass(mid)
        y_add(nz - 5, 2)
        y_dot(nz - 3, 2)
    else:
        y_add(0, 1)
        y_dot(1, 2)
    for d, u, sg, n in pairs:
        if n == half:
            drain(hall.at[nz - 1, sub(u)], ag_r.at[d, u, half - 1])
    y_dot(nz - 1, 1)
    y_add(nz - 3, 2)
    if big:
        cot_have(mid)
        part(2, 0)
    y_add(nz - 1, 1)
    if big:
        y_scatter(2)
        cot_have(near)
    else:
        for n in range(len(grps)):
            y_scatter(n)
        for n in range(4):
            dw(n)

    def out_two():
        drain(oB, oB_r)
        local(oB.at[p], out_v.at[tile(p)], ov_r).start()

        @pl.loop(1, nq)
        def _(k):
            q = qmod(p + k)
            remote(oB.at[q], out_v.at[tile(p)], ov_s, ov_r, qdev(q)).start()

    mids = [(2, functools.partial(y_finish, 0)), (2, functools.partial(y_finish, 1)),
            (3, functools.partial(y_finish, 2)), (3, functools.partial(dw, 0)), (4, functools.partial(dw, 1)),
            (4, functools.partial(dw, 2)), (5, functools.partial(dw, 3)), (6, out_two)]
    if not big:
        for n in range(len(grps)):
            y_finish(n)
        out_two()

    def rs_add(d, u, s):
        drain(rbuf.at[d, s - 1, sub(u)], rs_r.at[d, u, s - 1])
        sbuf[d, s, sub(u)] = (pbuf[lax.rem(s, 2), 1 - d, sub(u)]
                              + rbuf[d, s - 1, sub(u)].astype(F32)).astype(BF16)

    @pl.loop(2, half)
    def _(s):
        for d, u, sg, n in pairs:
            if n == half:
                @pl.when(s == 2)
                def _():
                    drain(rbuf.at[d, 0, sub(u)], rs_r.at[d, u, 0])
                    pbuf[0, 1 - d, sub(u)] += rbuf[d, 0, sub(u)].astype(F32)

            rs_add(d, u, s)
            rs(d, u, sg, s).start()

        @pl.when(s < half - 1)
        def _():
            part(s + 1, lax.rem(s + 1, 2))

        for at, fn in mids:
            pl.when(s == at)(fn)

    part_one(0)
    for d, u, sg, n in pairs:
        drain(rbuf.at[d, half - 1, sub(u)], rs_r.at[d, u, half - 1])
        if half == 2 and n == half:
            drain(rbuf.at[d, 0, sub(u)], rs_r.at[d, u, 0])
            pbuf[0, 0, sub(u)] += rbuf[d, 0, sub(u)].astype(F32)
        if d == 1:
            pbuf[0, 0, sub(u)] += (rbuf[0, half - 1, sub(u)].astype(F32)
                                   + rbuf[1, half - 1, sub(u)].astype(F32))
    local(pbuf.at[0, 0], dh_hbm, st.at[2]).start()
    drain(out_v, ov_r)
    local(out_v, out_hbm, st.at[3]).start()

    most = pl.ds(0, nz - 1)
    rest = pl.ds(0, nq - 1)
    drain(hall.at[most], ag_s)
    drain(hall.at[most], rs_s)
    drain(cA.at[rest], cA_s)
    drain(cB.at[most], cB_s)
    drain(call.at[rest, :, pl.ds(0, dw_h)], cg_s)
    drain(call.at[:, :, pl.ds(0, dw_h)], rel_s)
    drain(ysend, yp_s)
    drain(yrecv.at[rest], yr_s)
    drain(oB.at[most], oB_s)
    drain(oB.at[rest], ov_s)
    drain(accb.at[pl.ds(0, dw_h)], st.at[0])
    drain(accb.at[pl.ds(0, dw_h)], st.at[1])
    local(pbuf.at[0, 0], dh_hbm, st.at[2]).wait()
    local(out_v, out_hbm, st.at[3]).wait()


def finish(gate_ref, up_ref, mask_ref, outr_ref, dh_ref, dw_ref, out_ref, dgate_ref, dup_ref, ddown_ref):
    tok = gate_ref.shape[0]
    for r in range(0, tok, 32):
        rows = pl.ds(r, 32)
        dh = dh_ref[rows, :]
        g = gate_ref[rows, :].astype(F32)
        sig = 1.0 / (1.0 + jnp.exp(-g))
        dgate_ref[rows, :] = (dh * up_ref[rows, :].astype(F32) * sig * (1.0 + g * (1.0 - sig))).astype(BF16)
        dup_ref[rows, :] = (dh * (g * sig)).astype(BF16)
    br, bc = mask_ref.shape
    bs = dw_ref.shape[0] // br
    for i in range(br):
        for j in range(bc):
            sl = (pl.ds(i * bs, bs), pl.ds(j * bs, bs))
            keep = jnp.full((bs, bs), mask_ref[i, j], jnp.int32) > 0
            ddown_ref[sl] = jnp.where(keep, dw_ref[sl], jnp.zeros((bs, bs), BF16))
    out_ref[...] = outr_ref[...]


def body(nz, nq, gate_pre, up_pre, down_weight, block_mask, cotangent):
    tok, ffc = gate_pre.shape
    dr = down_weight.shape[0]
    dw_h = dr // 2
    half = nz // 2
    ng = len(groups(nz))
    dma = pltpu.SemaphoreType.DMA
    vm = pltpu.VMEM
    any_ = pl.BlockSpec(memory_space=pl.ANY)
    vmem = pl.BlockSpec(memory_space=pltpu.VMEM)
    smem = pl.BlockSpec(memory_space=pltpu.SMEM)
    outr, dh, dwr = pl.pallas_call(
        functools.partial(kernel, nz, nq),
        out_shape=(
            jax.ShapeDtypeStruct((tok, dw_h), BF16),
            jax.ShapeDtypeStruct((tok, ffc), F32),
            jax.ShapeDtypeStruct((dr, ffc), BF16),
        ),
        in_specs=[any_, any_, any_, smem, any_],
        out_specs=(any_,) * 3,
        scratch_shapes=[
            vm((tok, ffc), BF16), vm((tok, ffc), BF16), vm((dr, ffc), BF16), vm((tok, dw_h), BF16),
            vm((nz, tok, ffc), BF16), vm((nz, tok, dr), BF16),
            vm((nq, TR, TC), BF16), vm((nz, TR, TC), BF16),
            vm((nz, tok, dw_h), F32), vm((nz, tok, dw_h), BF16), vm((nz, tok, dw_h), BF16),
            vm((nz, tok, dw_h), BF16), vm((nq, nz, TR, TC), BF16),
            vm((nz, TR, TC), BF16), vm((nz, TR, TC), BF16), vm((tok, dw_h), BF16),
            vm((2, half, tok, ffc), BF16), vm((2, half, tok, ffc), BF16),
            vm((2, 2, tok, ffc), F32), vm((dr, ffc), F32), vm((dr, ffc), BF16),
            dma((5,)), dma, dma((2, SUB, half)), dma, dma((2, SUB, half)),
            dma, dma, dma, dma((3,)),
            dma, dma((3,)), dma, dma((3,)), dma, dma((nz,)), dma, dma((ng,)),
            dma, dma, dma, dma, dma((4,)), pltpu.SemaphoreType.REGULAR((2,)),
        ],
        compiler_params=pltpu.CompilerParams(
            collective_id=0, has_side_effects=True, vmem_limit_bytes=60 * 1024 * 1024),
    )(gate_pre, up_pre, down_weight, block_mask, cotangent)
    return pl.pallas_call(
        finish,
        out_shape=(
            jax.ShapeDtypeStruct((tok, dw_h), BF16),
            jax.ShapeDtypeStruct((tok, ffc), BF16),
            jax.ShapeDtypeStruct((tok, ffc), BF16),
            jax.ShapeDtypeStruct((dr, ffc), BF16),
        ),
        in_specs=[vmem, vmem, smem, vmem, vmem, vmem],
        out_specs=(vmem,) * 4,
    )(gate_pre, up_pre, block_mask, outr, dh, dwr)


def solution(mesh):
    nz = mesh.shape["row"]
    nq = mesh.shape["col"] // 2
    spec = P("row", "col")
    return jax.shard_map(functools.partial(body, nz, nq), mesh=mesh, in_specs=(spec,) * 5,
                         out_specs=(spec,) * 4, check_vma=False)
```

```python
import functools

import jax
import jax.numpy as jnp
from jax import lax
from jax.experimental import pallas as pl
from jax.experimental.pallas import tpu as pltpu
from jax.sharding import PartitionSpec as P

MESH = pl.DeviceIdType.MESH
SUB = 4
TR = 16
TC = 128
F32 = jnp.float32
BF16 = jnp.bfloat16


def nt_dot(a, b):
    return lax.dot_general(a, b, (((1,), (1,)), ((), ())), preferred_element_type=F32)


def tn_dot(a, b):
    return lax.dot_general(a, b, (((0,), (0,)), ((), ())), preferred_element_type=F32)


def groups(nz):
    half = nz // 2
    if half <= 4:
        return [(i, i + 1) for i in range(nz)]
    cut = [0, 3, nz - 5, nz]
    return list(zip(cut[:-1], cut[1:]))


def cot_groups(nz):
    half = nz // 2
    if half <= 4:
        return [(0, 1), (1, 2), (2, nz)]
    return [(0, half - 1), (half - 1, nz - 3), (nz - 3, nz)]


def kernel(nz, nq, gate_hbm, up_hbm, w_hbm, mask_hbm, cot_hbm,
           out_hbm, dh_hbm, dw_hbm,
           gate_v, up_v, wm, cot_v, hall, call, cA, cB,
           yown, ysend, yprt, ysum, yrecv, osum, oB, out_v,
           rbuf, sbuf, pbuf, acc, accb,
           ld, ag_s, ag_r, rs_s, rs_r, cA_s, cA_r, cB_s, cB_r,
           cg_s, cg_r, rel_s, rel_r, yp_s, yp_r, yr_s, yr_r,
           oB_s, oB_r, ov_s, ov_r, st, far_sem, mask_ref):
    z = lax.axis_index("row")
    col = lax.axis_index("col")
    p = lax.div(col, 2)
    c = lax.rem(col, 2)
    half = nz // 2
    tok, ffc = gate_v.shape
    dr = wm.shape[0]
    dw_h = dr // 2
    rsub = tok // SUB
    big = half > 4
    grps = groups(nz)
    cgrps = cot_groups(nz)

    def zdev(k):
        return (lax.rem(z + (k + nz), nz), col)

    def qmod(v):
        return lax.rem(v + nq, nq)

    def tile(q):
        return (pl.ds(pl.multiple_of(lax.div(q, 2) * TR, TR), TR),
                pl.ds(pl.multiple_of(lax.rem(q, 2) * TC, TC), TC))

    def qdev(q):
        return (z, q * 2 + c)

    pdev = (z, p * 2 + (1 - c))
    mine = pl.multiple_of(c * dw_h, TC)
    other = pl.multiple_of((1 - c) * dw_h, TC)

    def remote(src, dst, ss, rs, dev):
        return pltpu.make_async_remote_copy(
            src_ref=src, dst_ref=dst, send_sem=ss, recv_sem=rs,
            device_id=dev, device_id_type=MESH)

    def local(src, dst, sem):
        return pltpu.make_async_copy(src, dst, sem)

    def drain(ref, sem):
        pltpu.make_async_copy(ref, ref, sem).wait()

    bar = pltpu.get_barrier_semaphore()

    near_z = (1, -1, 2, -2) if big else range(1, nz)
    for k in near_z:
        pl.semaphore_signal(bar, inc=1, device_id=zdev(k), device_id_type=MESH)

    @pl.loop(1, nq)
    def _(k):
        pl.semaphore_signal(bar, inc=1, device_id=qdev(qmod(p + k)), device_id_type=MESH)

    pl.semaphore_signal(bar, inc=1, device_id=pdev, device_id_type=MESH)

    loads = [local(a, b, ld.at[i]) for i, (a, b) in enumerate((
        (gate_hbm, gate_v), (up_hbm, up_v), (cot_hbm, cot_v),
        (w_hbm.at[pl.ds(mine, dw_h)], wm.at[pl.ds(0, dw_h)]),
        (w_hbm.at[pl.ds(other, dw_h)], wm.at[pl.ds(dw_h, dw_h)]), (mask_hbm, mask_ref)))]
    for l in loads:
        l.start()
    loads[0].wait()
    loads[1].wait()
    g = gate_v[...].astype(F32)
    hall[0] = (g / (1.0 + jnp.exp(-g)) * up_v[...].astype(F32)).astype(BF16)
    for l in loads[2:]:
        l.wait()
    br, bc = mask_ref.shape
    bs = dr // br

    def keep_blocks(ref):
        for i in range(br):
            row = lax.rem(c * (br // 2) + i, br)
            for j in range(bc):
                sl = (pl.ds(i * bs, bs), pl.ds(j * bs, bs))
                keep = jnp.full((bs, bs), mask_ref[row, j], jnp.int32) > 0
                ref[sl] = jnp.where(keep, ref[sl], jnp.zeros((bs, bs), BF16))

    keep_blocks(wm)
    pl.semaphore_wait(bar, len(near_z) + nq)

    def tell(n):
        for k in (2 << n, -(2 << n)):
            pl.semaphore_signal(far_sem.at[n], inc=1, device_id=zdev(k), device_id_type=MESH)

    def hear(n):
        pl.semaphore_wait(far_sem.at[n], 2)

    if big:
        tell(0)

    def steps_of(d, u):
        return half if (u < SUB // 2) == (d == 0) else half - 1

    pairs = [(d, u, 1 - 2 * d, steps_of(d, u)) for u in range(SUB) for d in range(2)]

    def sub(u):
        return pl.ds(u * rsub, rsub)

    def held(d, s):
        return s * 2 - 1 + d

    def ag(d, u, sg, s, src=None, dst=None):
        src = held(d, s) if src is None else src
        dst = held(d, s + 1) if dst is None else dst
        return remote(hall.at[src, sub(u)], hall.at[dst, sub(u)], ag_s, ag_r.at[d, u, s], zdev(sg))

    def y_send(i, k):
        remote(ysend.at[pl.ds(i, k)], yprt.at[pl.ds(i, k)], yp_s, yp_r.at[i], pdev).start()

    def y_dot(i, k):
        v = nt_dot(hall[pl.ds(i, k)].reshape(k * tok, ffc), wm[...])
        ysend[pl.ds(i, k)] = v[:, dw_h:].astype(BF16).reshape(k, tok, dw_h)
        yown[pl.ds(i, k)] = v[:, :dw_h].reshape(k, tok, dw_h)
        y_send(i, k)

    def y_add(i, k):
        rows = pl.ds(i, k)
        drain(yprt.at[rows], yp_r.at[i])
        ysum[rows] = (yown[rows] + yprt[rows].astype(F32)).astype(BF16)

    def y_scatter(n, first=1, end=nq):
        lo, hi = grps[n]
        rows = pl.ds(lo, hi - lo)
        if first == 1:
            local(ysum.at[(rows,) + tile(p)], yrecv.at[p, rows], yr_r.at[n]).start()

        @pl.loop(first, end)
        def _(k):
            q = qmod(p + k)
            remote(ysum.at[(rows,) + tile(q)], yrecv.at[p, rows], yr_s, yr_r.at[n], qdev(q)).start()

    def y_finish(n):
        lo, hi = grps[n]
        rows = pl.ds(lo, hi - lo)
        drain(yrecv.at[:, rows], yr_r.at[n])
        osum[rows] = jnp.sum(yrecv[:, rows].astype(F32), axis=0).astype(BF16)
        for i in range(lo, hi):
            if i == 0:
                local(osum.at[0], oB.at[z], oB_r).start()
            else:
                off = -((i + 1) // 2) if i % 2 else i // 2
                remote(osum.at[i], oB.at[z], oB_s, oB_r, zdev(off)).start()

    def cot_one():
        local(cot_v.at[tile(p)], cA.at[p], cA_r).start()

        @pl.loop(1, nq)
        def _(k):
            q = qmod(p + k)
            remote(cot_v.at[tile(q)], cA.at[p], cA_s, cA_r, qdev(q)).start()

    def crows(n):
        return pl.ds(cgrps[n][0], cgrps[n][1] - cgrps[n][0])

    def cot_two():
        if big:
            hear(1)
        drain(cA, cA_r)
        local(cA.at[z], cB.at[0], cB_r.at[0]).start()
        for i in range(nz - 1, 0, -1):
            k = (i + 1) // 2 if i % 2 else -(i // 2)
            n = [lo <= i < hi for lo, hi in cgrps].index(True)
            dev = zdev(k)
            remote(cA.at[dev[0]], cB.at[i], cB_s, cB_r.at[n], dev).start()

    def cot_three(n, lo=1, hi=nq):
        rows = crows(n)
        dst = call.at[(rows,) + tile(p)]
        if lo == 1:
            drain(cB.at[rows], cB_r.at[n])
            local(cB.at[rows], dst, cg_r.at[n]).start()

        @pl.loop(lo, hi)
        def _(k):
            remote(cB.at[rows], dst, cg_s, cg_r.at[n], qdev(qmod(p + k))).start()

    def cot_pass(n):
        ref = call.at[crows(n), :, pl.ds(0, dw_h)]
        drain(ref, cg_r.at[n])
        remote(ref, call.at[crows(n), :, pl.ds(dw_h, dw_h)], rel_s, rel_r.at[n], pdev).start()

    def cot_have(n):
        drain(call.at[crows(n), :, pl.ds(dw_h, dw_h)], rel_r.at[n])

    def ag_far(d, u, sg, src):
        remote(hall.at[src, sub(u)], hall.at[nz - 1, sub(u)], ag_s, ag_r.at[d, u, half - 1], zdev(2 * sg)).start()

    cot_one()
    for d, u, sg, n in pairs:
        ag(d, u, sg, 0, src=0).start()
        if half == 2 and n == half:
            ag_far(d, u, sg, 0)
    if big:
        hear(0)
        tell(1)
    y_dot(0, 1)

    near, mid, far = 0, 1, 2
    last = SUB - 1
    cut = nq // 2
    events = [(1, last, cot_two), (2, last, functools.partial(y_scatter, 0)),
              (3, last, functools.partial(cot_three, near)),
              (4, last, functools.partial(cot_three, far)),
              (5, SUB // 4, functools.partial(cot_three, mid, 1, cut)),
              (5, SUB // 2, functools.partial(cot_three, mid, cut, nq)),
              (6, SUB // 4, functools.partial(y_scatter, 1, 1, cut)),
              (6, SUB // 2, functools.partial(y_scatter, 1, cut, nq)),
              (6, last, functools.partial(cot_pass, near)), (6, last, functools.partial(cot_pass, far))]

    @pl.loop(1, half - 1)
    def _(s):
        for d, u, sg, n in pairs:
            drain(hall.at[held(d, s), sub(u)], ag_r.at[d, u, s - 1])
            ag(d, u, sg, s).start()
            if n == half:
                @pl.when(s == half - 2)
                def _():
                    ag_far(d, u, sg, held(d, s))
            if u == 0 and d == 1:
                @pl.when(s == 1)
                def _():
                    y_add(0, 1)

                @pl.when(s > 1)
                def _():
                    y_add(2 * s - 3, 2)
            if d == 1:
                if u == last:
                    y_dot(2 * s - 1, 2)
                for at, on, fn in events:
                    if on == u:
                        pl.when(s == at)(fn)

    if not big:
        for at, on, fn in events:
            if getattr(fn, 'func', None) is not y_scatter:
                fn()
    for d, u, sg, n in pairs:
        drain(hall.at[held(d, half - 1), sub(u)], ag_r.at[d, u, half - 2])
    cot_have(far)

    def rs(d, u, sg, s):
        return remote(sbuf.at[d, s, sub(u)], rbuf.at[d, s, sub(u)], rs_s, rs_r.at[d, u, s], zdev(sg))

    def part(s, buf):
        m = half - s
        v = jnp.dot(call[pl.ds(2 * m - 1, 2)].reshape(2 * tok, dr), wm[...], preferred_element_type=F32)
        pbuf[buf] = v.reshape(2, tok, ffc)

    def part_one(i):
        pbuf[0, 0] = jnp.dot(call[i], wm[...], preferred_element_type=F32)

    def dw(n):
        lo, hi = n * nz // 4, (n + 1) * nz // 4
        v = tn_dot(call[lo:hi].reshape((hi - lo) * tok, dr), hall[lo:hi].reshape((hi - lo) * tok, ffc))
        if n == 0:
            acc[...] = v
        elif n < 3:
            acc[...] += v
        else:
            accb[...] = (acc[...] + v).astype(BF16)
            keep_blocks(accb)
            local(accb.at[pl.ds(0, dw_h)], dw_hbm.at[pl.ds(mine, dw_h)], st.at[0]).start()
            local(accb.at[pl.ds(dw_h, dw_h)], dw_hbm.at[pl.ds(other, dw_h)], st.at[1]).start()

    if not big:
        cot_pass(mid)
        cot_have(mid)
        cot_have(near)
    part_one(nz - 1)
    for d, u, sg, n in pairs:
        if n == half:
            sbuf[d, 0, sub(u)] = pbuf[0, 0, sub(u)].astype(BF16)
            remote(sbuf.at[d, 0, sub(u)], rbuf.at[d, 0, sub(u)], rs_s, rs_r.at[d, u, 0], zdev(2 * sg)).start()
    part(1, 1)
    for d, u, sg, n in pairs:
        sbuf[d, 1, sub(u)] = pbuf[1, 1 - d, sub(u)].astype(BF16)
        rs(d, u, sg, 1).start()
    if big:
        cot_pass(mid)
        y_add(nz - 5, 2)
        y_dot(nz - 3, 2)
    else:
        y_add(0, 1)
        y_dot(1, 2)
    for d, u, sg, n in pairs:
        if n == half:
            drain(hall.at[nz - 1, sub(u)], ag_r.at[d, u, half - 1])
    y_dot(nz - 1, 1)
    y_add(nz - 3, 2)
    if big:
        cot_have(mid)
        part(2, 0)
    y_add(nz - 1, 1)
    if big:
        y_scatter(2)
        cot_have(near)
    else:
        for n in range(len(grps)):
            y_scatter(n)
        for n in range(4):
            dw(n)

    def out_two():
        drain(oB, oB_r)
        local(oB.at[p], out_v.at[tile(p)], ov_r).start()

        @pl.loop(1, nq)
        def _(k):
            q = qmod(p + k)
            remote(oB.at[q], out_v.at[tile(p)], ov_s, ov_r, qdev(q)).start()

    mids = [(2, functools.partial(y_finish, 0)), (2, functools.partial(y_finish, 1)),
            (3, functools.partial(y_finish, 2)), (3, functools.partial(dw, 0)), (4, functools.partial(dw, 1)),
            (4, functools.partial(dw, 2)), (5, functools.partial(dw, 3)), (6, out_two)]
    if not big:
        for n in range(len(grps)):
            y_finish(n)
        out_two()

    def rs_add(d, u, s):
        drain(rbuf.at[d, s - 1, sub(u)], rs_r.at[d, u, s - 1])
        sbuf[d, s, sub(u)] = (pbuf[lax.rem(s, 2), 1 - d, sub(u)]
                              + rbuf[d, s - 1, sub(u)].astype(F32)).astype(BF16)

    @pl.loop(2, half)
    def _(s):
        for d, u, sg, n in pairs:
            if n == half:
                @pl.when(s == 2)
                def _():
                    drain(rbuf.at[d, 0, sub(u)], rs_r.at[d, u, 0])
                    pbuf[0, 1 - d, sub(u)] += rbuf[d, 0, sub(u)].astype(F32)

            rs_add(d, u, s)
            rs(d, u, sg, s).start()

        @pl.when(s < half - 1)
        def _():
            part(s + 1, lax.rem(s + 1, 2))

        for at, fn in mids:
            pl.when(s == at)(fn)

    part_one(0)
    for d, u, sg, n in pairs:
        drain(rbuf.at[d, half - 1, sub(u)], rs_r.at[d, u, half - 1])
        if half == 2 and n == half:
            drain(rbuf.at[d, 0, sub(u)], rs_r.at[d, u, 0])
            pbuf[0, 0, sub(u)] += rbuf[d, 0, sub(u)].astype(F32)
        if d == 1:
            pbuf[0, 0, sub(u)] += (rbuf[0, half - 1, sub(u)].astype(F32)
                                   + rbuf[1, half - 1, sub(u)].astype(F32))
    local(pbuf.at[0, 0], dh_hbm, st.at[2]).start()
    drain(out_v, ov_r)
    local(out_v, out_hbm, st.at[3]).start()

    most = pl.ds(0, nz - 1)
    rest = pl.ds(0, nq - 1)
    drain(hall.at[most], ag_s)
    drain(hall.at[most], rs_s)
    drain(cA.at[rest], cA_s)
    drain(cB.at[most], cB_s)
    drain(call.at[rest, :, pl.ds(0, dw_h)], cg_s)
    drain(call.at[:, :, pl.ds(0, dw_h)], rel_s)
    drain(ysend, yp_s)
    drain(yrecv.at[rest], yr_s)
    drain(oB.at[most], oB_s)
    drain(oB.at[rest], ov_s)
    drain(accb.at[pl.ds(0, dw_h)], st.at[0])
    drain(accb.at[pl.ds(0, dw_h)], st.at[1])
    local(pbuf.at[0, 0], dh_hbm, st.at[2]).wait()
    local(out_v, out_hbm, st.at[3]).wait()


def finish(gate_any, up_any, outr_any, dh_any, dw_any, out_any, dgate_any, dup_any, ddown_any,
           gate_v, up_v, dh_v, dgate_v, dup_v, sem):
    def copy(a, b, i):
        c = pltpu.make_async_copy(a, b, sem.at[i])
        c.start()
        return c

    loads = [copy(a, b, i) for i, (a, b) in enumerate(((gate_any, gate_v), (up_any, up_v), (dh_any, dh_v)))]
    stores = [copy(dw_any, ddown_any, 3), copy(outr_any, out_any, 4)]
    for l in loads:
        l.wait()
    tok = gate_v.shape[0]
    for r in range(0, tok, tok // 2):
        rows = pl.ds(r, tok // 2)
        dh = dh_v[rows, :]
        g = gate_v[rows, :].astype(F32)
        sig = 1.0 / (1.0 + jnp.exp(-g))
        dgate_v[rows, :] = (dh * up_v[rows, :].astype(F32) * sig * (1.0 + g * (1.0 - sig))).astype(BF16)
        dup_v[rows, :] = (dh * (g * sig)).astype(BF16)
    stores += [copy(dgate_v, dgate_any, 5), copy(dup_v, dup_any, 6)]
    for l in stores:
        l.wait()


def body(nz, nq, gate_pre, up_pre, down_weight, block_mask, cotangent):
    tok, ffc = gate_pre.shape
    dr = down_weight.shape[0]
    dw_h = dr // 2
    half = nz // 2
    ng = len(groups(nz))
    dma = pltpu.SemaphoreType.DMA
    vm = pltpu.VMEM
    any_ = pl.BlockSpec(memory_space=pl.ANY)
    hbm = pl.BlockSpec(memory_space=pltpu.HBM)
    pin = functools.partial(pltpu.with_memory_space_constraint, memory_space=pltpu.HBM)
    outr, dh, dwr = pl.pallas_call(
        functools.partial(kernel, nz, nq),
        out_shape=(
            jax.ShapeDtypeStruct((tok, dw_h), BF16),
            jax.ShapeDtypeStruct((tok, ffc), F32),
            jax.ShapeDtypeStruct((dr, ffc), BF16),
        ),
        in_specs=[hbm] * 5,
        out_specs=(any_,) * 3,
        scratch_shapes=[
            vm((tok, ffc), BF16), vm((tok, ffc), BF16), vm((dr, ffc), BF16), vm((tok, dw_h), BF16),
            vm((nz, tok, ffc), BF16), vm((nz, tok, dr), BF16),
            vm((nq, TR, TC), BF16), vm((nz, TR, TC), BF16),
            vm((nz, tok, dw_h), F32), vm((nz, tok, dw_h), BF16), vm((nz, tok, dw_h), BF16),
            vm((nz, tok, dw_h), BF16), vm((nq, nz, TR, TC), BF16),
            vm((nz, TR, TC), BF16), vm((nz, TR, TC), BF16), vm((tok, dw_h), BF16),
            vm((2, half, tok, ffc), BF16), vm((2, half, tok, ffc), BF16),
            vm((2, 2, tok, ffc), F32), vm((dr, ffc), F32), vm((dr, ffc), BF16),
            dma((6,)), dma, dma((2, SUB, half)), dma, dma((2, SUB, half)),
            dma, dma, dma, dma((3,)),
            dma, dma((3,)), dma, dma((3,)), dma, dma((nz,)), dma, dma((ng,)),
            dma, dma, dma, dma, dma((4,)), pltpu.SemaphoreType.REGULAR((2,)), pltpu.SMEM(block_mask.shape, jnp.int32),
        ],
        compiler_params=pltpu.CompilerParams(
            collective_id=0, has_side_effects=True, vmem_limit_bytes=24 * 1024 * 1024),
    )(pin(gate_pre), pin(up_pre), pin(down_weight), pin(block_mask), pin(cotangent))
    return pl.pallas_call(
        finish,
        out_shape=(
            jax.ShapeDtypeStruct((tok, dw_h), BF16),
            jax.ShapeDtypeStruct((tok, ffc), BF16),
            jax.ShapeDtypeStruct((tok, ffc), BF16),
            jax.ShapeDtypeStruct((dr, ffc), BF16),
        ),
        in_specs=[any_] * 5,
        out_specs=(any_,) * 4,
        scratch_shapes=[
            vm((tok, ffc), BF16), vm((tok, ffc), BF16), vm((tok, ffc), F32), vm((tok, ffc), BF16), vm((tok, ffc), BF16),
            dma((7,)),
        ],
        compiler_params=pltpu.CompilerParams(vmem_limit_bytes=8 * 1024 * 1024),
    )(gate_pre, up_pre, outr, dh, dwr)


def solution(mesh):
    nz = mesh.shape["row"]
    nq = mesh.shape["col"] // 2
    spec = P("row", "col")
    return jax.shard_map(functools.partial(body, nz, nq), mesh=mesh, in_specs=(spec,) * 5,
                         out_specs=(spec,) * 4, check_vma=False)
```

```python
import functools

import jax
import jax.numpy as jnp
from jax import lax
from jax.experimental import pallas as pl
from jax.experimental.pallas import tpu as pltpu
from jax.sharding import PartitionSpec as P

MESH = pl.DeviceIdType.MESH
SUB = 4
TR = 16
TC = 128
F32 = jnp.float32
BF16 = jnp.bfloat16


def nt_dot(a, b):
    return lax.dot_general(a, b, (((1,), (1,)), ((), ())), preferred_element_type=F32)


def tn_dot(a, b):
    return lax.dot_general(a, b, (((0,), (0,)), ((), ())), preferred_element_type=F32)


def groups(nz):
    half = nz // 2
    if half <= 4:
        return [(i, i + 1) for i in range(nz)]
    cut = [0, 3, nz - 5, nz]
    return list(zip(cut[:-1], cut[1:]))


def cot_groups(nz):
    half = nz // 2
    if half <= 4:
        return [(0, 1), (1, 2), (2, nz)]
    return [(0, half - 1), (half - 1, nz - 3), (nz - 3, nz)]


def kernel(nz, nq, gate_hbm, up_hbm, w_hbm, mask_hbm, cot_hbm,
           out_hbm, dh_hbm, dw_hbm,
           gate_v, up_v, wm, cot_v, hall, call, cA, cB,
           yown, ysend, yprt, ysum, yrecv, osum, oB, out_v,
           rbuf, sbuf, pbuf, acc, accb,
           ld, ag_s, ag_r, rs_s, rs_r, cA_s, cA_r, cB_s, cB_r,
           cg_s, cg_r, rel_s, rel_r, yp_s, yp_r, yr_s, yr_r,
           oB_s, oB_r, ov_s, ov_r, st, far_sem, mask_ref, plane_sem):
    z = lax.axis_index("row")
    col = lax.axis_index("col")
    p = lax.div(col, 2)
    c = lax.rem(col, 2)
    half = nz // 2
    tok, ffc = gate_v.shape
    dr = wm.shape[0]
    dw_h = dr // 2
    rsub = tok // SUB
    big = half > 4
    grps = groups(nz)
    cgrps = cot_groups(nz)

    def zdev(k):
        return (lax.rem(z + (k + nz), nz), col)

    def qmod(v):
        return lax.rem(v + nq, nq)

    def tile(q):
        return (pl.ds(pl.multiple_of(lax.div(q, 2) * TR, TR), TR),
                pl.ds(pl.multiple_of(lax.rem(q, 2) * TC, TC), TC))

    def qdev(q):
        return (z, q * 2 + c)

    pdev = (z, p * 2 + (1 - c))
    mine = pl.multiple_of(c * dw_h, TC)
    other = pl.multiple_of((1 - c) * dw_h, TC)

    def remote(src, dst, ss, rs, dev):
        return pltpu.make_async_remote_copy(
            src_ref=src, dst_ref=dst, send_sem=ss, recv_sem=rs,
            device_id=dev, device_id_type=MESH)

    def local(src, dst, sem):
        return pltpu.make_async_copy(src, dst, sem)

    def drain(ref, sem):
        pltpu.make_async_copy(ref, ref, sem).wait()

    bar = pltpu.get_barrier_semaphore()

    near_z = (1, -1, 2, -2) if big else range(1, nz)
    for k in near_z:
        pl.semaphore_signal(bar, inc=1, device_id=zdev(k), device_id_type=MESH)

    side = 4 if big else 2
    px, py = lax.div(p, side), lax.rem(p, side)
    for k in range(1, side):
        for q in (lax.rem(px + k, side) * side + py, px * side + lax.rem(py + k, side)):
            pl.semaphore_signal(bar, inc=1, device_id=qdev(q), device_id_type=MESH)

    pl.semaphore_signal(bar, inc=1, device_id=pdev, device_id_type=MESH)

    loads = [local(a, b, ld.at[i]) for i, (a, b) in enumerate((
        (gate_hbm, gate_v), (up_hbm, up_v), (cot_hbm, cot_v),
        (w_hbm.at[pl.ds(mine, dw_h)], wm.at[pl.ds(0, dw_h)]),
        (w_hbm.at[pl.ds(other, dw_h)], wm.at[pl.ds(dw_h, dw_h)]), (mask_hbm, mask_ref)))]
    for l in loads:
        l.start()
    loads[0].wait()
    loads[1].wait()
    g = gate_v[...].astype(F32)
    hall[0] = (g / (1.0 + jnp.exp(-g)) * up_v[...].astype(F32)).astype(BF16)
    for l in loads[2:]:
        l.wait()
    br, bc = mask_ref.shape
    bs = dr // br

    def keep_blocks(ref):
        for i in range(br):
            row = lax.rem(c * (br // 2) + i, br)
            for j in range(bc):
                sl = (pl.ds(i * bs, bs), pl.ds(j * bs, bs))
                keep = jnp.full((bs, bs), mask_ref[row, j], jnp.int32) > 0
                ref[sl] = jnp.where(keep, ref[sl], jnp.zeros((bs, bs), BF16))

    keep_blocks(wm)
    pl.semaphore_wait(bar, len(near_z) + 2 * (side - 1) + 1)
    for k in range(1, side):
        pl.semaphore_signal(plane_sem, inc=1, device_id=qdev(px * side + lax.rem(py + k, side)), device_id_type=MESH)

    def tell(n):
        for k in (2 << n, -(2 << n)):
            pl.semaphore_signal(far_sem.at[n], inc=1, device_id=zdev(k), device_id_type=MESH)

    def hear(n):
        pl.semaphore_wait(far_sem.at[n], 2)

    if big:
        tell(0)

    def steps_of(d, u):
        return half if (u < SUB // 2) == (d == 0) else half - 1

    pairs = [(d, u, 1 - 2 * d, steps_of(d, u)) for u in range(SUB) for d in range(2)]

    def sub(u):
        return pl.ds(u * rsub, rsub)

    def held(d, s):
        return s * 2 - 1 + d

    def ag(d, u, sg, s, src=None, dst=None):
        src = held(d, s) if src is None else src
        dst = held(d, s + 1) if dst is None else dst
        return remote(hall.at[src, sub(u)], hall.at[dst, sub(u)], ag_s, ag_r.at[d, u, s], zdev(sg))

    def y_send(i, k):
        remote(ysend.at[pl.ds(i, k)], yprt.at[pl.ds(i, k)], yp_s, yp_r.at[i], pdev).start()

    def y_dot(i, k):
        v = nt_dot(hall[pl.ds(i, k)].reshape(k * tok, ffc), wm[...])
        ysend[pl.ds(i, k)] = v[:, dw_h:].astype(BF16).reshape(k, tok, dw_h)
        yown[pl.ds(i, k)] = v[:, :dw_h].reshape(k, tok, dw_h)
        y_send(i, k)

    def y_add(i, k):
        rows = pl.ds(i, k)
        drain(yprt.at[rows], yp_r.at[i])
        ysum[rows] = (yown[rows] + yprt[rows].astype(F32)).astype(BF16)

    def y_scatter(n, first=1, end=nq):
        lo, hi = grps[n]
        rows = pl.ds(lo, hi - lo)
        if first == 1:
            local(ysum.at[(rows,) + tile(p)], yrecv.at[p, rows], yr_r.at[n]).start()

        @pl.loop(first, end)
        def _(k):
            q = qmod(p + k)
            remote(ysum.at[(rows,) + tile(q)], yrecv.at[p, rows], yr_s, yr_r.at[n], qdev(q)).start()

    def y_finish(n):
        lo, hi = grps[n]
        rows = pl.ds(lo, hi - lo)
        drain(yrecv.at[:, rows], yr_r.at[n])
        osum[rows] = jnp.sum(yrecv[:, rows].astype(F32), axis=0).astype(BF16)
        for i in range(lo, hi):
            if i == 0:
                local(osum.at[0], oB.at[z], oB_r).start()
            else:
                off = -((i + 1) // 2) if i % 2 else i // 2
                remote(osum.at[i], oB.at[z], oB_s, oB_r, zdev(off)).start()

    def cot_one():
        local(cot_v.at[tile(p)], cA.at[p], cA_r).start()

        @pl.loop(1, nq)
        def _(k):
            q = qmod(p + k)
            remote(cot_v.at[tile(q)], cA.at[p], cA_s, cA_r, qdev(q)).start()

    def crows(n):
        return pl.ds(cgrps[n][0], cgrps[n][1] - cgrps[n][0])

    def cot_two():
        if big:
            hear(1)
        drain(cA, cA_r)
        local(cA.at[z], cB.at[0], cB_r.at[0]).start()
        for i in range(nz - 1, 0, -1):
            k = (i + 1) // 2 if i % 2 else -(i // 2)
            n = [lo <= i < hi for lo, hi in cgrps].index(True)
            dev = zdev(k)
            remote(cA.at[dev[0]], cB.at[i], cB_s, cB_r.at[n], dev).start()

    def cot_three(n, lo=1, hi=nq):
        rows = crows(n)
        dst = call.at[(rows,) + tile(p)]
        if lo == 1:
            drain(cB.at[rows], cB_r.at[n])
            local(cB.at[rows], dst, cg_r.at[n]).start()

        @pl.loop(lo, hi)
        def _(k):
            remote(cB.at[rows], dst, cg_s, cg_r.at[n], qdev(qmod(p + k))).start()

    def cot_pass(n):
        ref = call.at[crows(n), :, pl.ds(0, dw_h)]
        drain(ref, cg_r.at[n])
        remote(ref, call.at[crows(n), :, pl.ds(dw_h, dw_h)], rel_s, rel_r.at[n], pdev).start()

    def cot_have(n):
        drain(call.at[crows(n), :, pl.ds(dw_h, dw_h)], rel_r.at[n])

    def ag_far(d, u, sg, src):
        remote(hall.at[src, sub(u)], hall.at[nz - 1, sub(u)], ag_s, ag_r.at[d, u, half - 1], zdev(2 * sg)).start()

    for d, u, sg, n in pairs:
        ag(d, u, sg, 0, src=0).start()
        if half == 2 and n == half:
            ag_far(d, u, sg, 0)
    pl.semaphore_wait(plane_sem, side - 1)
    cot_one()
    if big:
        hear(0)
        tell(1)
    y_dot(0, 1)

    near, mid, far = 0, 1, 2
    last = SUB - 1
    cut = nq // 2
    events = [(1, last, cot_two), (2, last, functools.partial(y_scatter, 0)),
              (3, last, functools.partial(cot_three, near)),
              (4, last, functools.partial(cot_three, far)),
              (5, SUB // 4, functools.partial(cot_three, mid, 1, cut)),
              (5, SUB // 2, functools.partial(cot_three, mid, cut, nq)),
              (6, SUB // 4, functools.partial(y_scatter, 1, 1, cut)),
              (6, SUB // 2, functools.partial(y_scatter, 1, cut, nq)),
              (6, last, functools.partial(cot_pass, near)), (6, last, functools.partial(cot_pass, far))]

    @pl.loop(1, half - 1)
    def _(s):
        for d, u, sg, n in pairs:
            drain(hall.at[held(d, s), sub(u)], ag_r.at[d, u, s - 1])
            ag(d, u, sg, s).start()
            if n == half:
                @pl.when(s == half - 2)
                def _():
                    ag_far(d, u, sg, held(d, s))
            if u == 0 and d == 1:
                @pl.when(s == 1)
                def _():
                    y_add(0, 1)

                @pl.when(s > 1)
                def _():
                    y_add(2 * s - 3, 2)
            if d == 1:
                if u == last:
                    y_dot(2 * s - 1, 2)
                for at, on, fn in events:
                    if on == u:
                        pl.when(s == at)(fn)

    if not big:
        for at, on, fn in events:
            if getattr(fn, 'func', None) is not y_scatter:
                fn()
    for d, u, sg, n in pairs:
        drain(hall.at[held(d, half - 1), sub(u)], ag_r.at[d, u, half - 2])
    cot_have(far)

    def rs(d, u, sg, s):
        return remote(sbuf.at[d, s, sub(u)], rbuf.at[d, s, sub(u)], rs_s, rs_r.at[d, u, s], zdev(sg))

    def part(s, buf):
        m = half - s
        v = jnp.dot(call[pl.ds(2 * m - 1, 2)].reshape(2 * tok, dr), wm[...], preferred_element_type=F32)
        pbuf[buf] = v.reshape(2, tok, ffc)

    def part_one(i):
        pbuf[0, 0] = jnp.dot(call[i], wm[...], preferred_element_type=F32)

    def dw(n):
        lo, hi = n * nz // 4, (n + 1) * nz // 4
        v = tn_dot(call[lo:hi].reshape((hi - lo) * tok, dr), hall[lo:hi].reshape((hi - lo) * tok, ffc))
        if n == 0:
            acc[...] = v
        elif n < 3:
            acc[...] += v
        else:
            accb[...] = (acc[...] + v).astype(BF16)
            keep_blocks(accb)
            local(accb.at[pl.ds(0, dw_h)], dw_hbm.at[pl.ds(mine, dw_h)], st.at[0]).start()
            local(accb.at[pl.ds(dw_h, dw_h)], dw_hbm.at[pl.ds(other, dw_h)], st.at[1]).start()

    if not big:
        cot_pass(mid)
        cot_have(mid)
        cot_have(near)
    part_one(nz - 1)
    for d, u, sg, n in pairs:
        if n == half:
            sbuf[d, 0, sub(u)] = pbuf[0, 0, sub(u)].astype(BF16)
            remote(sbuf.at[d, 0, sub(u)], rbuf.at[d, 0, sub(u)], rs_s, rs_r.at[d, u, 0], zdev(2 * sg)).start()
    part(1, 1)
    for d, u, sg, n in pairs:
        sbuf[d, 1, sub(u)] = pbuf[1, 1 - d, sub(u)].astype(BF16)
        rs(d, u, sg, 1).start()
    if big:
        cot_pass(mid)
        y_add(nz - 5, 2)
        y_dot(nz - 3, 2)
    else:
        y_add(0, 1)
        y_dot(1, 2)
    for d, u, sg, n in pairs:
        if n == half:
            drain(hall.at[nz - 1, sub(u)], ag_r.at[d, u, half - 1])
    y_dot(nz - 1, 1)
    y_add(nz - 3, 2)
    if big:
        cot_have(mid)
        part(2, 0)
    y_add(nz - 1, 1)
    if big:
        y_scatter(2)
        cot_have(near)
    else:
        for n in range(len(grps)):
            y_scatter(n)
        for n in range(4):
            dw(n)

    def out_two():
        drain(oB, oB_r)
        local(oB.at[p], out_v.at[tile(p)], ov_r).start()

        @pl.loop(1, nq)
        def _(k):
            q = qmod(p + k)
            remote(oB.at[q], out_v.at[tile(p)], ov_s, ov_r, qdev(q)).start()

    mids = [(2, functools.partial(y_finish, 0)), (2, functools.partial(y_finish, 1)),
            (3, functools.partial(y_finish, 2)), (3, functools.partial(dw, 0)), (4, functools.partial(dw, 1)),
            (4, functools.partial(dw, 2)), (5, functools.partial(dw, 3)), (6, out_two)]
    if not big:
        for n in range(len(grps)):
            y_finish(n)
        out_two()

    def rs_add(d, u, s):
        drain(rbuf.at[d, s - 1, sub(u)], rs_r.at[d, u, s - 1])
        sbuf[d, s, sub(u)] = (pbuf[lax.rem(s, 2), 1 - d, sub(u)]
                              + rbuf[d, s - 1, sub(u)].astype(F32)).astype(BF16)

    @pl.loop(2, half)
    def _(s):
        for d, u, sg, n in pairs:
            if n == half:
                @pl.when(s == 2)
                def _():
                    drain(rbuf.at[d, 0, sub(u)], rs_r.at[d, u, 0])
                    pbuf[0, 1 - d, sub(u)] += rbuf[d, 0, sub(u)].astype(F32)

            rs_add(d, u, s)
            rs(d, u, sg, s).start()

        @pl.when(s < half - 1)
        def _():
            part(s + 1, lax.rem(s + 1, 2))

        for at, fn in mids:
            pl.when(s == at)(fn)

    part_one(0)
    for d, u, sg, n in pairs:
        drain(rbuf.at[d, half - 1, sub(u)], rs_r.at[d, u, half - 1])
        if half == 2 and n == half:
            drain(rbuf.at[d, 0, sub(u)], rs_r.at[d, u, 0])
            pbuf[0, 0, sub(u)] += rbuf[d, 0, sub(u)].astype(F32)
        if d == 1:
            pbuf[0, 0, sub(u)] += (rbuf[0, half - 1, sub(u)].astype(F32)
                                   + rbuf[1, half - 1, sub(u)].astype(F32))
    local(pbuf.at[0, 0], dh_hbm, st.at[2]).start()
    drain(out_v, ov_r)
    local(out_v, out_hbm, st.at[3]).start()

    most = pl.ds(0, nz - 1)
    rest = pl.ds(0, nq - 1)
    drain(hall.at[most], ag_s)
    drain(hall.at[most], rs_s)
    drain(cA.at[rest], cA_s)
    drain(cB.at[most], cB_s)
    drain(call.at[rest, :, pl.ds(0, dw_h)], cg_s)
    drain(call.at[:, :, pl.ds(0, dw_h)], rel_s)
    drain(ysend, yp_s)
    drain(yrecv.at[rest], yr_s)
    drain(oB.at[most], oB_s)
    drain(oB.at[rest], ov_s)
    drain(accb.at[pl.ds(0, dw_h)], st.at[0])
    drain(accb.at[pl.ds(0, dw_h)], st.at[1])
    local(pbuf.at[0, 0], dh_hbm, st.at[2]).wait()
    local(out_v, out_hbm, st.at[3]).wait()


def finish(gate_any, up_any, outr_any, dh_any, dw_any, out_any, dgate_any, dup_any, ddown_any,
           gate_v, up_v, dh_v, dgate_v, dup_v, sem):
    def copy(a, b, i):
        c = pltpu.make_async_copy(a, b, sem.at[i])
        c.start()
        return c

    loads = [copy(a, b, i) for i, (a, b) in enumerate(((gate_any, gate_v), (up_any, up_v), (dh_any, dh_v)))]
    stores = [copy(dw_any, ddown_any, 3), copy(outr_any, out_any, 4)]
    for l in loads:
        l.wait()
    tok = gate_v.shape[0]
    for r in range(0, tok, tok // 2):
        rows = pl.ds(r, tok // 2)
        dh = dh_v[rows, :]
        g = gate_v[rows, :].astype(F32)
        sig = 1.0 / (1.0 + jnp.exp(-g))
        dgate_v[rows, :] = (dh * up_v[rows, :].astype(F32) * sig * (1.0 + g * (1.0 - sig))).astype(BF16)
        dup_v[rows, :] = (dh * (g * sig)).astype(BF16)
    stores += [copy(dgate_v, dgate_any, 5), copy(dup_v, dup_any, 6)]
    for l in stores:
        l.wait()


def body(nz, nq, gate_pre, up_pre, down_weight, block_mask, cotangent):
    tok, ffc = gate_pre.shape
    dr = down_weight.shape[0]
    dw_h = dr // 2
    half = nz // 2
    ng = len(groups(nz))
    dma = pltpu.SemaphoreType.DMA
    vm = pltpu.VMEM
    any_ = pl.BlockSpec(memory_space=pl.ANY)
    hbm = pl.BlockSpec(memory_space=pltpu.HBM)
    pin = functools.partial(pltpu.with_memory_space_constraint, memory_space=pltpu.HBM)
    outr, dh, dwr = pl.pallas_call(
        functools.partial(kernel, nz, nq),
        out_shape=(
            jax.ShapeDtypeStruct((tok, dw_h), BF16),
            jax.ShapeDtypeStruct((tok, ffc), F32),
            jax.ShapeDtypeStruct((dr, ffc), BF16),
        ),
        in_specs=[hbm] * 5,
        out_specs=(any_,) * 3,
        scratch_shapes=[
            vm((tok, ffc), BF16), vm((tok, ffc), BF16), vm((dr, ffc), BF16), vm((tok, dw_h), BF16),
            vm((nz, tok, ffc), BF16), vm((nz, tok, dr), BF16),
            vm((nq, TR, TC), BF16), vm((nz, TR, TC), BF16),
            vm((nz, tok, dw_h), F32), vm((nz, tok, dw_h), BF16), vm((nz, tok, dw_h), BF16),
            vm((nz, tok, dw_h), BF16), vm((nq, nz, TR, TC), BF16),
            vm((nz, TR, TC), BF16), vm((nz, TR, TC), BF16), vm((tok, dw_h), BF16),
            vm((2, half, tok, ffc), BF16), vm((2, half, tok, ffc), BF16),
            vm((2, 2, tok, ffc), F32), vm((dr, ffc), F32), vm((dr, ffc), BF16),
            dma((6,)), dma, dma((2, SUB, half)), dma, dma((2, SUB, half)),
            dma, dma, dma, dma((3,)),
            dma, dma((3,)), dma, dma((3,)), dma, dma((nz,)), dma, dma((ng,)),
            dma, dma, dma, dma, dma((4,)), pltpu.SemaphoreType.REGULAR((2,)), pltpu.SMEM(block_mask.shape, jnp.int32),
            pltpu.SemaphoreType.REGULAR,
        ],
        compiler_params=pltpu.CompilerParams(
            collective_id=0, has_side_effects=True, vmem_limit_bytes=24 * 1024 * 1024),
    )(pin(gate_pre), pin(up_pre), pin(down_weight), pin(block_mask), pin(cotangent))
    return pl.pallas_call(
        finish,
        out_shape=(
            jax.ShapeDtypeStruct((tok, dw_h), BF16),
            jax.ShapeDtypeStruct((tok, ffc), BF16),
            jax.ShapeDtypeStruct((tok, ffc), BF16),
            jax.ShapeDtypeStruct((dr, ffc), BF16),
        ),
        in_specs=[any_] * 5,
        out_specs=(any_,) * 4,
        scratch_shapes=[
            vm((tok, ffc), BF16), vm((tok, ffc), BF16), vm((tok, ffc), F32), vm((tok, ffc), BF16), vm((tok, ffc), BF16),
            dma((7,)),
        ],
        compiler_params=pltpu.CompilerParams(vmem_limit_bytes=8 * 1024 * 1024),
    )(gate_pre, up_pre, outr, dh, dwr)


def solution(mesh):
    nz = mesh.shape["row"]
    nq = mesh.shape["col"] // 2
    spec = P("row", "col")
    return jax.shard_map(functools.partial(body, nz, nq), mesh=mesh, in_specs=(spec,) * 5,
                         out_specs=(spec,) * 4, check_vma=False)
```
